256 devices in a mesh: space: 64 (over z, x, core), inst: 4 (over y).
Axes of the slice: x: 4, y: 4, z: 8, core: 2. Of those that a mesh axis runs over, the one named last changes fastest.
Arguments:
- adjoint: float32 [8, 5, 131072], P('inst', None, 'space'), may hold values from -6 to 6
- jac_cell: float32 [8, 5, 5, 131072], P('inst', None, None, 'space'), may hold values from -2.5 to 2.5
- jac_left: float32 [8, 5, 5, 131072], P('inst', None, None, 'space'), may hold values from -2.5 to 2.5
- jac_right: float32 [8, 5, 5, 131072], P('inst', None, None, 'space'), may hold values from -2.5 to 2.5
- volume: float32 [131072], P('space'), may hold values from 0.5 to 2
- normals: float32 [3, 131072], P(None, 'space'), may hold values from -6 to 6
- surface: int32 [131072], P('space'), may hold values 0 or 1
- instance_map: int32 [8], replicated, may hold values from 0 to 7, each once
- mode_shapes: float32 [200, 3, 131072], P(None, None, 'space'), may hold values from -0.01953125 to 0.01953125
- damping: float32 [200], replicated, may hold values from 0.2 to 2
- modal_inverse: float32 [200, 200], replicated, may hold values from -2 to 3
Outputs:
- flow_residual: float32 [8, 5, 131072], P('inst', None, 'space')
- mesh_forcing: float32 [8, 3, 131072], P('inst', None, 'space')
- modal_adjoint: float32 [8, 200], P('inst')
The draws below stay inside these ranges and needn't reach their ends.
All inputs are finite; a program needn't handle non-finite values. No bound on the sum of `surface` on one device may be relied on, other than what follows from the above.
Results may differ from the reference program's by a relative error of at most 0.000068.
Values sent between devices are 32-bit elements; how exact they have to be, the bound alone decides.
A program may use at most 64 MiB of HBM per device.

```python
import math
import jax
import jax.numpy as jnp
from jax import lax

NI = 8
MODES = 200
NCELLS = 131072


def draw_modal_inverse(key, part):
    first, second = jax.random.split(key)
    diagonal = jnp.exp(jax.random.uniform(first, (MODES,), jnp.float32, math.log(0.5), math.log(2.0)))
    spread = jax.random.normal(second, (MODES, MODES), jnp.float32) * (0.5 / math.sqrt(MODES))
    spread = jnp.clip(spread, -0.9, 0.9)
    return jnp.eye(MODES, dtype=jnp.float32) * diagonal[:, None] + spread


def set_ends(entries, stream_key, low, top_value):
    place = [jax.random.randint(jax.random.fold_in(stream_key, axis), (), 0, length) for axis, length in enumerate(entries.shape)]
    widest = entries.shape.index(max(entries.shape))
    neighbour = place[:widest] + [(place[widest] + 1) % entries.shape[widest]] + place[widest + 1:]
    return entries.at[tuple(place)].set(low).at[tuple(neighbour)].set(top_value)


def level_of(rng, dims, pieces, least, top_value):
    def one(axis_at, shards_of):
        draws = jax.random.uniform(jax.random.fold_in(jax.random.fold_in(rng, 6), axis_at), (shards_of,), jnp.float32, least / len(pieces), top_value / len(pieces))
        return jnp.repeat(jnp.exp(draws), dims[axis_at] // shards_of).reshape((-1,) + (1,) * (len(dims) - axis_at - 1))

    gain = one(*pieces[0])
    for cut in pieces[1:]:
        gain = gain * one(*cut)
    return gain


def bell_draw(own_key, extent, scale, most, cuts=(), kind=jnp.bfloat16):
    values = jax.random.normal(own_key, extent, jnp.float32) * scale
    if len(cuts) > 0:
        values = level_of(own_key, extent, cuts, -0.22, 0.18) * values
    return jnp.clip(values, min=-most, max=most).astype(kind)


def setup_inputs(seed: int = 0) -> dict:
    arg_keys = jax.random.split(jax.random.key(seed), 12)
    return {
        "adjoint": bell_draw(arg_keys[0], (NI, 5, NCELLS), 1.0, 6.0, ((0, 4), (2, 64)), jnp.float32),
        "jac_cell": bell_draw(arg_keys[1], (NI, 5, 5, NCELLS), 5 ** -0.5, 2.5, ((0, 4), (3, 64)), jnp.float32),
        "jac_left": bell_draw(arg_keys[2], (NI, 5, 5, NCELLS), 5 ** -0.5, 2.5, ((0, 4), (3, 64)), jnp.float32),
        "jac_right": bell_draw(arg_keys[3], (NI, 5, 5, NCELLS), 5 ** -0.5, 2.5, ((0, 4), (3, 64)), jnp.float32),
        "volume": jnp.clip(jnp.exp(math.log(2.0) - 1.3862944 * jax.random.uniform(arg_keys[4], (NCELLS,), jnp.float32) ** level_of(arg_keys[4], (NCELLS,), ((0, 64),), -0.2, 0.2)), 0.5, 2.0),
        "normals": bell_draw(arg_keys[5], (3, NCELLS), 1.0, 6.0, ((1, 64),), jnp.float32),
        "surface": set_ends((jax.random.randint(arg_keys[6], (NCELLS,), 0, 4) < 1).astype(jnp.int32), jax.random.fold_in(arg_keys[6], 1), 0, 1),
        "instance_map": jax.random.permutation(arg_keys[7], NI).astype(jnp.int32),
        "mode_shapes": bell_draw(arg_keys[8], (MODES, 3, NCELLS), (3 * NCELLS // 4) ** -0.5, 0.01953125, ((2, 64),), jnp.float32),
        "damping": jnp.clip(jnp.exp(jax.random.uniform(arg_keys[9], (MODES,), jnp.float32, math.log(0.2), math.log(2.0))), 0.2, 2.0),
        "modal_inverse": draw_modal_inverse(jax.random.fold_in(arg_keys[11], 71), 0),
    }


def coupling_matrix(instance_map):
    count = instance_map.shape[0]
    slots = instance_map.astype(jnp.float32)
    differ = slots[:, None] - slots[None, :]
    angle = jnp.pi * differ / count
    same = differ == 0
    sine = jnp.where(same, 1.0, jnp.sin(angle))
    return jnp.where(same, 0.0, 0.5 * jnp.cos(jnp.pi * differ) * jnp.cos(angle) / sine).astype(jnp.float32)


def reference(adjoint, jac_cell, jac_left, jac_right, volume, normals, surface, instance_map, mode_shapes, damping, modal_inverse):
    highest = lax.Precision.HIGHEST
    flow = jnp.einsum("sfec,sfc->sec", jac_cell, adjoint, precision=highest)
    from_left = jnp.einsum("sfec,sfc->sec", jac_left, adjoint, precision=highest)
    from_right = jnp.einsum("sfec,sfc->sec", jac_right, adjoint, precision=highest)
    zeros = jnp.zeros_like(from_left[:, :, :1])
    flow = flow + jnp.concatenate([from_left[:, :, 1:], zeros], axis=2)
    flow = flow + jnp.concatenate([zeros, from_right[:, :, :-1]], axis=2)
    coupling = coupling_matrix(instance_map)
    timed = jnp.einsum("ab,aec->bec", coupling, adjoint, precision=highest)
    flow = flow + volume[None, None, :] * timed
    walls = surface.astype(jnp.float32)
    force = (walls[None, :] * flow[:, 4, :])[:, None, :] * normals[None, :, :]
    shapes = mode_shapes.reshape(MODES, -1)
    projected = lax.dot_general(force.reshape(NI, -1), shapes, (((1,), (1,)), ((), ())), precision=highest, preferred_element_type=jnp.float32)
    modal_rhs = projected + damping[None, :] * jnp.dot(coupling.T, projected, precision=highest)
    modal_adjoint = jnp.dot(modal_rhs, modal_inverse, precision=highest)
    expanded = jnp.dot(modal_adjoint, shapes, precision=highest).reshape(NI, 3, -1)
    mesh_forcing = walls[None, None, :] * expanded
    return flow, mesh_forcing, modal_adjoint
```

```python
import jax
import jax.numpy as jnp
from jax import lax
from jax.experimental import pallas as pl
from jax.experimental.pallas import tpu as pltpu
from jax.sharding import PartitionSpec as P

MESH = pl.DeviceIdType.MESH
HIGHEST = lax.Precision.HIGHEST
F32 = jnp.float32

NZ, NX, NY, NC = 8, 4, 4, 2
TILES = NZ * NX * NC
CHIPS = NZ * NX
MODES = 200
GROUPS = MODES // 8
ROWS = 208
WIDE = 256
CT = 16
CHUNKS = 4
CJ = CT // CHUNKS
MB = 5
EJ = 4


def iota(shape, dim):
    return lax.broadcasted_iota(jnp.int32, shape, dim)


def next_cell(x):
    shape = x.shape
    rolled = pltpu.roll(x, 127, 1)
    carried = pltpu.roll(rolled, shape[0] - 2, 0)
    carried = jnp.where(iota(shape, 0) >= shape[0] - 2, 0.0, carried)
    return jnp.where(iota(shape, 1) == 127, carried, rolled)


def previous_cell(x):
    shape = x.shape
    rolled = pltpu.roll(x, 1, 1)
    carried = pltpu.roll(rolled, 2, 0)
    carried = jnp.where(iota(shape, 0) < 2, 0.0, carried)
    return jnp.where(iota(shape, 1) == 0, carried, rolled)


def coupling_of(differ):
    d = differ.astype(F32)
    angle = d * (jnp.pi / 8)
    same = differ == 0
    sine = jnp.where(same, 1.0, jnp.sin(angle))
    return jnp.where(same, 0.0, 0.5 * jnp.cos(jnp.pi * d) * jnp.cos(angle) / sine)


def kernel(
    adj_h, jc_h, jl_h, jr_h, vol_h, nrm_h, surf_h, imap_h, shp_h, damp_h, inv_h,
    flow_o, mesh_o, modal_o,
    adj, jac4, jac, vol, nrm, surf, imap, shp, damp, inv,
    ls, vol2, surf2, ng, wts, acc, fl, fr, fb, hmat,
    ma, abuf, vmsg, vbuf, xl, xp, mb, bbuf, rr, inv_t, coef,
    hl, hr,
    lsem, csem, ready,
    asend, arecv, vsend, vrecv, hsend, hrecv, gsend, grecv, bsend, brecv,
):
    space, y = lax.axis_index("space"), lax.axis_index("inst")
    core = lax.rem(space, NC)
    chip = space // NC
    x = lax.rem(chip, NX)
    z = chip // NX
    other = 1 - core

    def at(zz, xx, cc):
        return (zz * NX + xx) * NC + cc

    local = []

    def bring(src, dst, sem):
        copy = pltpu.make_async_copy(src, dst, sem)
        copy.start()
        local.append(copy)
        return copy

    c_adj = bring(adj_h, adj.at[y], lsem.at[0])
    c_j4 = [bring(j.at[:, 4], jac4.at[i], lsem.at[1 + i]) for i, j in enumerate((jc_h, jl_h, jr_h))]
    c_vol = bring(vol_h, vol, lsem.at[4])
    c_surf = bring(surf_h, surf, lsem.at[5])
    c_nrm = bring(nrm_h, nrm, lsem.at[6])
    c_shp = []
    for k in range(CHUNKS):
        part = pl.ds(k * CJ * 128, CJ * 128)
        copy = pltpu.make_async_copy(shp_h.at[:, :, part], shp.at[:, :, part], csem.at[k])
        copy.start()
        c_shp.append(copy)
    c_imap = bring(imap_h, imap, lsem.at[7])
    c_damp = bring(damp_h, damp, lsem.at[8])
    c_inv = bring(inv_h, inv, lsem.at[9])
    c_jac = [bring(j.at[:, pl.ds(0, 4)], jac.at[i], lsem.at[10 + i]) for i, j in enumerate((jc_h, jl_h, jr_h))]

    barrier = pltpu.get_barrier_semaphore()

    def greet(where, inst):
        pl.semaphore_signal(barrier, inc=1, device_id=(where, inst), device_id_type=MESH)

    for dy in range(1, NY):
        for cc in range(NC):
            greet(at(z, x, cc), lax.rem(y + dy, NY))
    for dx in range(1, NX):
        for cc in range(NC):
            greet(at(z, lax.rem(x + dx, NX), cc), y)
    for dz in range(1, NZ):
        for cc in range(NC):
            greet(at(lax.rem(z + dz, NZ), x, cc), y)
    greet(at(z, x, other), y)
    greet(lax.rem(chip + CHIPS - 1, CHIPS) * NC + 1, y)
    greet(lax.rem(chip + 1, CHIPS) * NC, y)
    greeted = (NY - 1) * NC + (NX - 1) * NC + (NZ - 1) * NC + 3

    ma[...] = jnp.zeros_like(ma)
    vmsg[...] = jnp.zeros_like(vmsg)
    acc[...] = jnp.zeros_like(acc)

    c_vol.wait()
    c_surf.wait()
    c_nrm.wait()
    walls = surf[...].astype(F32)
    for s in range(2):
        vol2[pl.ds(s, CT, stride=2), :] = vol[...]
        surf2[pl.ds(s, CT, stride=2), :] = walls
    for d in range(3):
        for j in range(CT):
            ng[d, pl.ds(j, 1), :] = nrm[pl.ds(d, 1), pl.ds(128 * j, 128)]
    for d in range(3):
        ng[d] = ng[d] * walls
    c_adj.wait()
    for c in c_j4:
        c.wait()

    def combine(j, e):
        total = j[0, e] * adj[y, 0]
        for f in range(1, 5):
            total = total + j[f, e] * adj[y, f]
        return total

    def direct4(i):
        total = jac4[i, 0] * adj[y, 0]
        for f in range(1, 5):
            total = total + jac4[i, f] * adj[y, f]
        return total

    left4, right4 = direct4(1), direct4(2)
    fl[4] = left4
    fr[4] = right4
    base4 = direct4(0) + next_cell(left4) + previous_cell(right4)
    fb[4] = base4
    ls[0] = base4
    ls[1] = vol2[...] * adj[y, 4]
    for r in range(4):
        rows = ls[r // 2, pl.ds(r % 2, CT, stride=2), :]
        for d in range(3):
            wts[r, pl.ds(d * CT, CT), :] = rows * ng[d]
    lane8, sub8 = iota((8, 128), 1), iota((8, 128), 0)
    first = jnp.where(lane8 == 0, left4[0:8], 0.0)
    last = jnp.where(lane8 == 127, right4[24:32], 0.0)
    for s in range(2):
        edge = jnp.where(sub8 == 0, pltpu.roll(first, (8 - s) % 8, 0), 0.0)
        edge = edge + jnp.where(sub8 == 1, pltpu.roll(last, 3 - s, 0), 0.0)
        acc[s, pl.ds(MODES, 8), :] = edge

    for k in range(CHUNKS):
        c_shp[k].wait()

        def block(g, carry, k=k):
            row = pl.multiple_of(g * (8 * MB), 8)
            sums = [[acc[r, pl.ds(row + 8 * i, 8), :] for i in range(MB)] for r in range(4)]
            for d in range(3):
                for jj in range(CJ):
                    j = k * CJ + jj
                    weight = [wts[r, pl.ds(d * CT + j, 8, stride=0), :] for r in range(4)]
                    for i in range(MB):
                        tile = shp[d, pl.ds(row + 8 * i, 8), pl.ds(128 * j, 128)]
                        for r in range(4):
                            sums[r][i] = sums[r][i] + weight[r] * tile
            for r in range(4):
                for i in range(MB):
                    acc[r, pl.ds(row + 8 * i, 8), :] = sums[r][i]
            return carry

        lax.fori_loop(0, GROUPS // MB, block, 0)
    ends = ((0, 0), (CT - 1, 127))
    for v, (j, lane) in enumerate(ends):
        total = None
        for d in range(3):
            g = jnp.where(iota((1, 128), 1) == lane, ng[d, pl.ds(j, 1), :], 0.0)
            term = shp[d, :, pl.ds(128 * j, 128)] * g
            total = term if total is None else total + term
        acc[4 + v, pl.ds(0, MODES), :] = total
    ones = jnp.ones((8, 128), F32)
    across = (((1,), (1,)), ((), ()))
    for r in range(6):
        summed = lax.dot_general(ones, acc[r], across, precision=HIGHEST, preferred_element_type=F32)
        if r < 4:
            ma[pl.ds(r, 1), pl.ds(0, ROWS)] = summed[0:1]
        else:
            vmsg[pl.ds(r - 4, 1), pl.ds(0, ROWS)] = summed[0:1]

    pl.semaphore_wait(barrier, greeted)
    for dx in range(1, NX):
        for cc in range(NC):
            pl.semaphore_signal(ready, inc=1, device_id=(at(z, lax.rem(x + dx, NX), cc), y), device_id_type=MESH)

    def send(src, dst, ssem, rsem, where, inst):
        copy = pltpu.make_async_remote_copy(
            src_ref=src, dst_ref=dst, send_sem=ssem, recv_sem=rsem, device_id=(where, inst), device_id_type=MESH
        )
        copy.start()
        return copy

    mine = y * NC + core
    sent_a = []
    for n in range(1, NY * NC):
        dy, dc = n // NC, n % NC
        cc = lax.rem(core + dc, NC)
        sent_a.append(send(ma, abuf.at[mine], asend.at[n], arecv.at[mine], at(z, x, cc), lax.rem(y + dy, NY)))
    sent_v = [send(vmsg, vbuf.at[core], vsend.at[0], vrecv.at[core], at(z, x, other), y)]
    outer = lax.rem(chip + 2 * core - 1 + CHIPS, CHIPS)
    slot = 3 - core
    for cc in range(NC):
        sent_v.append(send(vmsg, vbuf.at[slot], vsend.at[1 + cc], vrecv.at[slot], outer * NC + cc, y))
    sent_g = []
    for dy in range(1, NY):
        sent_g.append(send(adj.at[y], adj.at[y], gsend.at[dy], grecv.at[y], space, lax.rem(y + dy, NY)))
    abuf[pl.ds(mine, 1)] = ma[...][None]
    vbuf[pl.ds(core, 1)] = vmsg[...][None]

    for c in c_jac:
        c.wait()

    def component(e, carry):
        left, right = combine(jac.at[1], e), combine(jac.at[2], e)
        fl[e] = left
        fr[e] = right
        fb[e] = combine(jac.at[0], e) + next_cell(left) + previous_cell(right)
        return carry

    lax.fori_loop(0, 4, component, 0)
    before, after = lax.rem(space + TILES - 1, TILES), lax.rem(space + 1, TILES)
    sent_h = [
        send(fl.at[:, pl.ds(0, 8), :], hr, hsend.at[0], hrecv.at[0], before, y),
        send(fr.at[:, pl.ds(24, 8), :], hl, hsend.at[1], hrecv.at[1], after, y),
    ]

    c_imap.wait()
    c_damp.wait()
    c_inv.wait()
    eight = iota((8, 8), 0) == iota((8, 8), 1)
    slots = jnp.broadcast_to(imap[...], (8, 8))
    down = jnp.sum(jnp.where(eight, slots.astype(F32), 0.0), axis=1, keepdims=True)
    differ = jnp.broadcast_to(down, (8, 8)) - slots.astype(F32)
    hmat[...] = coupling_of(differ.astype(jnp.int32))
    h = hmat[...]
    own = 2 * y + core
    rows8 = iota((8, 8), 0)
    lanes8 = iota((8, 8), 1)
    own_h = jnp.sum(jnp.where(lanes8 == own, h, 0.0), axis=1, keepdims=True)
    inv_t[...] = inv[...].T

    for n in range(1, NY * NC):
        dy, dc = n // NC, n % NC
        src = lax.rem(y + dy, NY) * NC + lax.rem(core + dc, NC)
        pltpu.make_async_copy(ma, abuf.at[src], arecv.at[src]).wait()
    pltpu.make_async_copy(vmsg, vbuf.at[other], vrecv.at[other]).wait()
    for v in (2, 3):
        pltpu.make_async_copy(vmsg, vbuf.at[v], vrecv.at[v]).wait()
    for cc in range(NC):
        for yy in range(NY):
            xl[cc, pl.ds(2 * yy, 2), :] = abuf[yy * NC + cc, pl.ds(0, 2), :]
            xp[cc, pl.ds(2 * yy, 2), :] = abuf[yy * NC + cc, pl.ds(2, 2), :]
    has_before = jnp.where(chip > 0, 1.0, 0.0)
    has_after = jnp.where(chip < CHIPS - 1, 1.0, 0.0)
    proj = xl[0] + xl[1]
    edges = (
        (xl[0][:, 200:201] * has_before, vbuf[2, pl.ds(1, 1), :]),
        (xl[0][:, 201:202], vbuf[1, pl.ds(0, 1), :]),
        (xl[1][:, 200:201], vbuf[0, pl.ds(1, 1), :]),
        (xl[1][:, 201:202] * has_after, vbuf[3, pl.ds(0, 1), :]),
    )
    for amount, vector in edges:
        proj = proj + amount * vector
    late = xp[0] + xp[1]
    for a in range(8):
        proj = proj - h[:, a : a + 1] * late[a : a + 1, :]
    plain = jnp.sum(jnp.where(iota((8, WIDE), 0) == own, proj, 0.0), axis=0, keepdims=True)
    mixed = jnp.sum(own_h * proj, axis=0, keepdims=True)
    rhs = plain[:, 0:MODES] + damp[...] * mixed[:, 0:MODES]
    mb[...] = jnp.zeros_like(mb)
    mb[pl.ds(0, 1), :] = rhs[:, 0:128]
    mb[pl.ds(1, 1), pl.ds(0, MODES - 128)] = rhs[:, 128:MODES]

    pl.semaphore_wait(ready, (NX - 1) * NC)

    def send_b(n, carry):
        send(mb, bbuf.at[space], bsend.at[n], brecv.at[space], lax.rem(space + n, TILES), y)
        return carry

    lax.fori_loop(1, TILES, send_b, 0)
    bbuf[pl.ds(space, 1)] = mb[...][None]

    pltpu.make_async_copy(hr, hr, hrecv.at[0]).wait()
    pltpu.make_async_copy(hl, hl, hrecv.at[1]).wait()
    for dy in range(1, NY):
        src = lax.rem(y + dy, NY)
        pltpu.make_async_copy(adj.at[src], adj.at[src], grecv.at[src]).wait()
    parity = lax.rem(iota((8, 128), 0), 2)
    pick = [jnp.sum(jnp.where(lanes8 == 2 * y + s, h, 0.0), axis=1, keepdims=True) for s in range(2)]

    def entry(a, s):
        return jnp.broadcast_to(pick[s][a : a + 1, :], (8, 128))

    same = [jnp.where(parity == 0, entry(2 * yy, 0), entry(2 * yy + 1, 1)) for yy in range(NY)]
    cross = [jnp.where(parity == 0, entry(2 * yy + 1, 0), entry(2 * yy, 1)) for yy in range(NY)]
    follows = jnp.where(space < TILES - 1, 1.0, 0.0)
    leads = jnp.where(space > 0, 1.0, 0.0)

    def finish(e, carry):
        for q in range(4):
            part = pl.ds(8 * q, 8)
            timed = jnp.zeros((8, 128), F32)
            for yy in range(NY):
                here = adj[yy, e, part, :]
                swapped = jnp.where(parity == 0, pltpu.roll(here, 7, 0), pltpu.roll(here, 1, 0))
                timed = timed + here * same[yy] + swapped * cross[yy]
            total = fb[e, part, :] + vol2[part, :] * timed
            if q == 0:
                moved = pltpu.roll(pltpu.roll(hl[e], 1, 1), 2, 0)
                total = total + jnp.where((sub8 < 2) & (lane8 == 0), moved * leads, 0.0)
            if q == 3:
                moved = pltpu.roll(pltpu.roll(hr[e], 127, 1), 6, 0)
                total = total + jnp.where((sub8 >= 6) & (lane8 == 127), moved * follows, 0.0)
            flow_o[e, part, :] = total
        return carry

    lax.fori_loop(0, 5, finish, 0)
    for c in sent_a + sent_v + sent_g + sent_h:
        c.wait_send()

    def arrive(n, carry):
        src = lax.rem(space + n, TILES)
        pltpu.make_async_copy(mb, bbuf.at[src], brecv.at[src]).wait()
        return carry

    lax.fori_loop(1, TILES, arrive, 0)
    rr[...] = jnp.zeros_like(rr)
    for cc in range(NC):
        total = bbuf[cc]
        for n in range(1, CHIPS):
            total = total + bbuf[n * NC + cc]
        rr[pl.ds(cc, 1), pl.ds(0, 128)] = total[0:1]
        rr[pl.ds(cc, 1), pl.ds(128, 128)] = total[1:2]
    both = rr[:, pl.ds(0, MODES)]
    columns = lax.dot_general(inv_t[...], both, across, precision=HIGHEST, preferred_element_type=F32)
    for s in range(2):
        coef[s] = jnp.broadcast_to(columns[:, s : s + 1], (MODES, 128))

    def expand(n, carry):
        d = n // (CT // EJ)
        j0 = lax.rem(n, CT // EJ) * EJ
        sums = [[jnp.zeros((8, 128), F32) for _ in range(EJ)] for _ in range(2)]
        for g in range(GROUPS):
            c0, c1 = coef[0, pl.ds(8 * g, 8), :], coef[1, pl.ds(8 * g, 8), :]
            for i in range(EJ):
                tile = shp[d, pl.ds(8 * g, 8), pl.ds(pl.multiple_of((j0 + i) * 128, 128), 128)]
                sums[0][i] = sums[0][i] + c0 * tile
                sums[1][i] = sums[1][i] + c1 * tile
        for i in range(EJ):
            for s in range(2):
                row = 2 * (j0 + i) + s
                line = jnp.sum(sums[s][i], axis=0, keepdims=True)
                mesh_o[d, pl.ds(row, 1), :] = line * surf2[pl.ds(row, 1), :]
        return carry

    lax.fori_loop(0, 3 * (CT // EJ), expand, 0)
    modal = jnp.dot(both, inv[...], precision=HIGHEST, preferred_element_type=F32)
    modal_o[...] = modal[0:2]

    def drain(n, carry):
        pltpu.make_async_copy(mb, mb, bsend.at[n]).wait()
        return carry

    lax.fori_loop(1, TILES, drain, 0)


def shards(
    adjoint, jac_cell, jac_left, jac_right, volume, normals, surface, instance_map, mode_shapes, damping, modal_inverse
):
    def tiles(array):
        lead = array.shape[1:-1]
        n = len(lead)
        split = array.reshape((2,) + lead + (CT, 128))
        order = tuple(range(1, n + 1)) + (n + 1, 0, n + 2)
        return split.transpose(order).reshape(lead + (2 * CT, 128))

    def slots(array):
        lead = array.shape[0]
        return array.reshape(lead, CT, 2, 128).transpose(2, 0, 1, 3).reshape(2, lead, CT * 128)

    args = (
        tiles(adjoint),
        tiles(jac_cell),
        tiles(jac_left),
        tiles(jac_right),
        volume.reshape(CT, 128),
        normals,
        surface.reshape(CT, 128),
        instance_map.reshape(1, 8),
        mode_shapes.transpose(1, 0, 2),
        damping.reshape(1, MODES),
        modal_inverse,
    )
    vmem = pltpu.VMEM
    dma = pltpu.SemaphoreType.DMA
    flow, mesh, modal = pl.pallas_call(
        kernel,
        out_shape=(
            jax.ShapeDtypeStruct((5, 2 * CT, 128), F32),
            jax.ShapeDtypeStruct((3, 2 * CT, 128), F32),
            jax.ShapeDtypeStruct((2, MODES), F32),
        ),
        in_specs=[pl.BlockSpec(memory_space=pl.ANY)] * len(args),
        out_specs=[pl.BlockSpec(memory_space=pltpu.VMEM)] * 3,
        scratch_shapes=[
            vmem((NY, 5, 32, 128), F32),
            vmem((3, 5, 32, 128), F32),
            vmem((3, 5, 4, 32, 128), F32),
            vmem((CT, 128), F32),
            vmem((3, CT * 128), F32),
            vmem((CT, 128), jnp.int32),
            vmem((1, 8), jnp.int32),
            vmem((3, MODES, CT * 128), F32),
            vmem((1, MODES), F32),
            vmem((MODES, MODES), F32),
            vmem((2, 32, 128), F32),
            vmem((32, 128), F32),
            vmem((32, 128), F32),
            vmem((3, CT, 128), F32),
            vmem((4, 3 * CT, 128), F32),
            vmem((6, ROWS, 128), F32),
            vmem((5, 32, 128), F32),
            vmem((5, 32, 128), F32),
            vmem((5, 32, 128), F32),
            vmem((8, 8), F32),
            vmem((4, WIDE), F32),
            vmem((NY * NC, 4, WIDE), F32),
            vmem((2, WIDE), F32),
            vmem((4, 2, WIDE), F32),
            vmem((2, 8, WIDE), F32),
            vmem((2, 8, WIDE), F32),
            vmem((2, 128), F32),
            vmem((TILES, 2, 128), F32),
            vmem((8, WIDE), F32),
            vmem((MODES, MODES), F32),
            vmem((2, MODES, 128), F32),
            vmem((5, 8, 128), F32),
            vmem((5, 8, 128), F32),
            dma((13,)),
            dma((CHUNKS,)),
            pltpu.SemaphoreType.REGULAR,
            dma((NY * NC,)),
            dma((NY * NC,)),
            dma((3,)),
            dma((4,)),
            dma((2,)),
            dma((2,)),
            dma((NY,)),
            dma((NY,)),
            dma((TILES,)),
            dma((TILES,)),
        ],
        compiler_params=pltpu.CompilerParams(
            collective_id=0, has_side_effects=True, vmem_limit_bytes=48 * 1024 * 1024
        ),
    )(*args)
    return slots(flow), slots(mesh), modal


def solution(mesh):
    placed = (
        P("inst", None, "space"),
        P("inst", None, None, "space"),
        P("inst", None, None, "space"),
        P("inst", None, None, "space"),
        P("space"),
        P(None, "space"),
        P("space"),
        P(),
        P(None, None, "space"),
        P(),
        P(),
    )
    return jax.shard_map(
        shards,
        mesh=mesh,
        in_specs=placed,
        out_specs=(P("inst", None, "space"), P("inst", None, "space"), P("inst", None)),
        check_vma=False,
    )
```

```python
import jax
import jax.numpy as jnp
from jax import lax
from jax.experimental import pallas as pl
from jax.experimental.pallas import tpu as pltpu
from jax.sharding import PartitionSpec as P

MESH = pl.DeviceIdType.MESH
HIGHEST = lax.Precision.HIGHEST
F32 = jnp.float32

NZ, NX, NY, NC = 8, 4, 4, 2
TILES = NZ * NX * NC
CHIPS = NZ * NX
MODES = 200
GROUPS = MODES // 8
ROWS = 208
WIDE = 256
CT = 16
CHUNKS = 8
AHEAD = 4
CJ = CT // CHUNKS
MB = 5
EJ = 4


def iota(shape, dim):
    return lax.broadcasted_iota(jnp.int32, shape, dim)


def next_cell(x):
    shape = x.shape
    rolled = pltpu.roll(x, 127, 1)
    carried = pltpu.roll(rolled, shape[0] - 2, 0)
    carried = jnp.where(iota(shape, 0) >= shape[0] - 2, 0.0, carried)
    return jnp.where(iota(shape, 1) == 127, carried, rolled)


def previous_cell(x):
    shape = x.shape
    rolled = pltpu.roll(x, 1, 1)
    carried = pltpu.roll(rolled, 2, 0)
    carried = jnp.where(iota(shape, 0) < 2, 0.0, carried)
    return jnp.where(iota(shape, 1) == 0, carried, rolled)


def coupling_of(differ):
    d = differ.astype(F32)
    angle = d * (jnp.pi / 8)
    same = differ == 0
    sine = jnp.where(same, 1.0, jnp.sin(angle))
    return jnp.where(same, 0.0, 0.5 * jnp.cos(jnp.pi * d) * jnp.cos(angle) / sine)


def kernel(
    adj_h, jc_h, jl_h, jr_h, vol_h, nrm_h, surf_h, imap_h, shp_h, damp_h, inv_h,
    flow_o, mesh_o, modal_o,
    adj, jac4, jac, vol, nrm, surf, imap, shp, damp, inv,
    ls, vol2, surf2, ng, wts, acc, fl, fr, fb, hmat,
    ma, abuf, vmsg, vbuf, xl, xp, mb, bbuf, rr, inv_t, coef,
    hl, hr,
    lsem, csem, ready,
    asend, arecv, vsend, vrecv, hsend, hrecv, gsend, grecv, bsend, brecv,
):
    space, y = lax.axis_index("space"), lax.axis_index("inst")
    core = lax.rem(space, NC)
    chip = space // NC
    x = lax.rem(chip, NX)
    z = chip // NX
    other = 1 - core

    def at(zz, xx, cc):
        return (zz * NX + xx) * NC + cc

    local = []

    def bring(src, dst, sem):
        copy = pltpu.make_async_copy(src, dst, sem)
        copy.start()
        local.append(copy)
        return copy

    c_adj = bring(adj_h, adj.at[y], lsem.at[0])
    c_j4 = [bring(j.at[:, 4], jac4.at[i], lsem.at[1 + i]) for i, j in enumerate((jc_h, jl_h, jr_h))]
    c_vol = bring(vol_h, vol, lsem.at[4])
    c_surf = bring(surf_h, surf, lsem.at[5])
    c_nrm = bring(nrm_h, nrm, lsem.at[6])

    def chunk(k):
        part = pl.ds(pl.multiple_of(k * (CJ * 128), CJ * 128), CJ * 128)
        return pltpu.make_async_copy(shp_h.at[:, :, part], shp.at[:, :, part], csem.at[k])

    for k in range(AHEAD):
        chunk(k).start()

    barrier = pltpu.get_barrier_semaphore()

    def greet(where, inst):
        pl.semaphore_signal(barrier, inc=1, device_id=(where, inst), device_id_type=MESH)

    for dy in range(1, NY):
        for cc in range(NC):
            greet(at(z, x, cc), lax.rem(y + dy, NY))
    for dx in range(1, NX):
        for cc in range(NC):
            greet(at(z, lax.rem(x + dx, NX), cc), y)
    for dz in range(1, NZ):
        for cc in range(NC):
            greet(at(lax.rem(z + dz, NZ), x, cc), y)
    greet(at(z, x, other), y)
    greet(lax.rem(chip + CHIPS - 1, CHIPS) * NC + 1, y)
    greet(lax.rem(chip + 1, CHIPS) * NC, y)
    greeted = (NY - 1) * NC + (NX - 1) * NC + (NZ - 1) * NC + 3

    ma[...] = jnp.zeros_like(ma)
    vmsg[...] = jnp.zeros_like(vmsg)
    acc[...] = jnp.zeros_like(acc)

    c_vol.wait()
    c_surf.wait()
    c_nrm.wait()
    walls = surf[...].astype(F32)
    for s in range(2):
        vol2[pl.ds(s, CT, stride=2), :] = vol[...]
        surf2[pl.ds(s, CT, stride=2), :] = walls
    for d in range(3):
        for j in range(CT):
            ng[d, pl.ds(j, 1), :] = nrm[pl.ds(d, 1), pl.ds(128 * j, 128)]
    for d in range(3):
        ng[d] = ng[d] * walls
    c_adj.wait()
    for c in c_j4:
        c.wait()

    def combine(j, e):
        total = j[0, e] * adj[y, 0]
        for f in range(1, 5):
            total = total + j[f, e] * adj[y, f]
        return total

    def direct4(i):
        total = jac4[i, 0] * adj[y, 0]
        for f in range(1, 5):
            total = total + jac4[i, f] * adj[y, f]
        return total

    left4, right4 = direct4(1), direct4(2)
    fl[4] = left4
    fr[4] = right4
    base4 = direct4(0) + next_cell(left4) + previous_cell(right4)
    fb[4] = base4
    ls[0] = base4
    ls[1] = vol2[...] * adj[y, 4]
    for r in range(4):
        rows = ls[r // 2, pl.ds(r % 2, CT, stride=2), :]
        for d in range(3):
            wts[r, pl.ds(d * CT, CT), :] = rows * ng[d]
    lane8, sub8 = iota((8, 128), 1), iota((8, 128), 0)
    first = jnp.where(lane8 == 0, left4[0:8], 0.0)
    last = jnp.where(lane8 == 127, right4[24:32], 0.0)
    for s in range(2):
        edge = jnp.where(sub8 == 0, pltpu.roll(first, (8 - s) % 8, 0), 0.0)
        edge = edge + jnp.where(sub8 == 1, pltpu.roll(last, 3 - s, 0), 0.0)
        acc[s, pl.ds(MODES, 8), :] = edge

    def project(k, carry):
        chunk(k).wait()

        @pl.when(k + AHEAD < CHUNKS)
        def _():
            chunk(k + AHEAD).start()

        def block(g, carry):
            row = pl.multiple_of(g * (8 * MB), 8)
            sums = [[acc[r, pl.ds(row + 8 * i, 8), :] for i in range(MB)] for r in range(4)]
            for d in range(3):
                for jj in range(CJ):
                    j = k * CJ + jj
                    weight = [wts[r, pl.ds(d * CT + j, 8, stride=0), :] for r in range(4)]
                    column = pl.ds(pl.multiple_of(128 * j, 128), 128)
                    for i in range(MB):
                        tile = shp[d, pl.ds(row + 8 * i, 8), column]
                        for r in range(4):
                            sums[r][i] = sums[r][i] + weight[r] * tile
            for r in range(4):
                for i in range(MB):
                    acc[r, pl.ds(row + 8 * i, 8), :] = sums[r][i]
            return carry

        return lax.fori_loop(0, GROUPS // MB, block, carry)

    lax.fori_loop(0, CHUNKS, project, 0)
    c_imap = bring(imap_h, imap, lsem.at[7])
    c_damp = bring(damp_h, damp, lsem.at[8])
    c_inv = bring(inv_h, inv, lsem.at[9])
    c_jac = [bring(j.at[:, pl.ds(0, 4)], jac.at[i], lsem.at[10 + i]) for i, j in enumerate((jc_h, jl_h, jr_h))]
    ends = ((0, 0), (CT - 1, 127))
    for v, (j, lane) in enumerate(ends):
        total = None
        for d in range(3):
            g = jnp.where(iota((1, 128), 1) == lane, ng[d, pl.ds(j, 1), :], 0.0)
            term = shp[d, :, pl.ds(128 * j, 128)] * g
            total = term if total is None else total + term
        acc[4 + v, pl.ds(0, MODES), :] = total
    ones = jnp.ones((8, 128), F32)
    across = (((1,), (1,)), ((), ()))
    for r in range(6):
        summed = lax.dot_general(ones, acc[r], across, precision=HIGHEST, preferred_element_type=F32)
        if r < 4:
            ma[pl.ds(r, 1), pl.ds(0, ROWS)] = summed[0:1]
        else:
            vmsg[pl.ds(r - 4, 1), pl.ds(0, ROWS)] = summed[0:1]

    pl.semaphore_wait(barrier, greeted)
    for dx in range(1, NX):
        for cc in range(NC):
            pl.semaphore_signal(ready, inc=1, device_id=(at(z, lax.rem(x + dx, NX), cc), y), device_id_type=MESH)

    def send(src, dst, ssem, rsem, where, inst):
        copy = pltpu.make_async_remote_copy(
            src_ref=src, dst_ref=dst, send_sem=ssem, recv_sem=rsem, device_id=(where, inst), device_id_type=MESH
        )
        copy.start()
        return copy

    mine = y * NC + core
    sent_a = []
    for dy, dc in ((2, 0), (2, 1), (1, 0), (3, 0), (1, 1), (3, 1), (0, 1)):
        n = dy * NC + dc
        cc = lax.rem(core + dc, NC)
        sent_a.append(send(ma, abuf.at[mine], asend.at[n], arecv.at[mine], at(z, x, cc), lax.rem(y + dy, NY)))
    sent_v = [send(vmsg, vbuf.at[core], vsend.at[0], vrecv.at[core], at(z, x, other), y)]
    outer = lax.rem(chip + 2 * core - 1 + CHIPS, CHIPS)
    slot = 3 - core
    for cc in range(NC):
        sent_v.append(send(vmsg, vbuf.at[slot], vsend.at[1 + cc], vrecv.at[slot], outer * NC + cc, y))
    sent_g = []
    for dy in range(1, NY):
        sent_g.append(send(adj.at[y], adj.at[y], gsend.at[dy], grecv.at[y], space, lax.rem(y + dy, NY)))
    abuf[pl.ds(mine, 1)] = ma[...][None]
    vbuf[pl.ds(core, 1)] = vmsg[...][None]

    for c in c_jac:
        c.wait()

    def component(e, carry):
        left, right = combine(jac.at[1], e), combine(jac.at[2], e)
        fl[e] = left
        fr[e] = right
        fb[e] = combine(jac.at[0], e) + next_cell(left) + previous_cell(right)
        return carry

    lax.fori_loop(0, 4, component, 0)
    before, after = lax.rem(space + TILES - 1, TILES), lax.rem(space + 1, TILES)
    sent_h = [
        send(fl.at[:, pl.ds(0, 8), :], hr, hsend.at[0], hrecv.at[0], before, y),
        send(fr.at[:, pl.ds(24, 8), :], hl, hsend.at[1], hrecv.at[1], after, y),
    ]

    c_imap.wait()
    c_damp.wait()
    c_inv.wait()
    eight = iota((8, 8), 0) == iota((8, 8), 1)
    slots = jnp.broadcast_to(imap[...], (8, 8))
    down = jnp.sum(jnp.where(eight, slots.astype(F32), 0.0), axis=1, keepdims=True)
    differ = jnp.broadcast_to(down, (8, 8)) - slots.astype(F32)
    hmat[...] = coupling_of(differ.astype(jnp.int32))
    h = hmat[...]
    own = 2 * y + core
    rows8 = iota((8, 8), 0)
    lanes8 = iota((8, 8), 1)
    own_h = jnp.sum(jnp.where(lanes8 == own, h, 0.0), axis=1, keepdims=True)
    inv_t[...] = inv[...].T

    for n in range(1, NY * NC):
        dy, dc = n // NC, n % NC
        src = lax.rem(y + dy, NY) * NC + lax.rem(core + dc, NC)
        pltpu.make_async_copy(ma, abuf.at[src], arecv.at[src]).wait()
    pltpu.make_async_copy(vmsg, vbuf.at[other], vrecv.at[other]).wait()
    for v in (2, 3):
        pltpu.make_async_copy(vmsg, vbuf.at[v], vrecv.at[v]).wait()
    for cc in range(NC):
        for yy in range(NY):
            xl[cc, pl.ds(2 * yy, 2), :] = abuf[yy * NC + cc, pl.ds(0, 2), :]
            xp[cc, pl.ds(2 * yy, 2), :] = abuf[yy * NC + cc, pl.ds(2, 2), :]
    has_before = jnp.where(chip > 0, 1.0, 0.0)
    has_after = jnp.where(chip < CHIPS - 1, 1.0, 0.0)
    proj = xl[0] + xl[1]
    edges = (
        (xl[0][:, 200:201] * has_before, vbuf[2, pl.ds(1, 1), :]),
        (xl[0][:, 201:202], vbuf[1, pl.ds(0, 1), :]),
        (xl[1][:, 200:201], vbuf[0, pl.ds(1, 1), :]),
        (xl[1][:, 201:202] * has_after, vbuf[3, pl.ds(0, 1), :]),
    )
    for amount, vector in edges:
        proj = proj + amount * vector
    late = xp[0] + xp[1]
    for a in range(8):
        proj = proj - h[:, a : a + 1] * late[a : a + 1, :]
    plain = jnp.sum(jnp.where(iota((8, WIDE), 0) == own, proj, 0.0), axis=0, keepdims=True)
    mixed = jnp.sum(own_h * proj, axis=0, keepdims=True)
    rhs = plain[:, 0:MODES] + damp[...] * mixed[:, 0:MODES]
    mb[...] = jnp.zeros_like(mb)
    mb[pl.ds(0, 1), :] = rhs[:, 0:128]
    mb[pl.ds(1, 1), pl.ds(0, MODES - 128)] = rhs[:, 128:MODES]

    pl.semaphore_wait(ready, (NX - 1) * NC)

    def hops(offset):
        dz, dx, _ = offset
        return min(dz, NZ - dz) + min(dx, NX - dx)

    offsets = [(dz, dx, dc) for dz in range(NZ) for dx in range(NX) for dc in range(NC)][1:]
    for n, (dz, dx, dc) in enumerate(sorted(offsets, key=hops, reverse=True)):
        where = at(lax.rem(z + dz, NZ), lax.rem(x + dx, NX), lax.rem(core + dc, NC))
        send(mb, bbuf.at[space], bsend.at[n], brecv.at[space], where, y)
    bbuf[pl.ds(space, 1)] = mb[...][None]

    pltpu.make_async_copy(hr, hr, hrecv.at[0]).wait()
    pltpu.make_async_copy(hl, hl, hrecv.at[1]).wait()
    for dy in range(1, NY):
        src = lax.rem(y + dy, NY)
        pltpu.make_async_copy(adj.at[src], adj.at[src], grecv.at[src]).wait()
    parity = lax.rem(iota((8, 128), 0), 2)
    pick = [jnp.sum(jnp.where(lanes8 == 2 * y + s, h, 0.0), axis=1, keepdims=True) for s in range(2)]

    def entry(a, s):
        return jnp.broadcast_to(pick[s][a : a + 1, :], (8, 128))

    same = [jnp.where(parity == 0, entry(2 * yy, 0), entry(2 * yy + 1, 1)) for yy in range(NY)]
    cross = [jnp.where(parity == 0, entry(2 * yy + 1, 0), entry(2 * yy, 1)) for yy in range(NY)]
    follows = jnp.where(space < TILES - 1, 1.0, 0.0)
    leads = jnp.where(space > 0, 1.0, 0.0)

    def finish(e, carry):
        for q in range(4):
            part = pl.ds(8 * q, 8)
            timed = jnp.zeros((8, 128), F32)
            for yy in range(NY):
                here = adj[yy, e, part, :]
                swapped = jnp.where(parity == 0, pltpu.roll(here, 7, 0), pltpu.roll(here, 1, 0))
                timed = timed + here * same[yy] + swapped * cross[yy]
            total = fb[e, part, :] + vol2[part, :] * timed
            if q == 0:
                moved = pltpu.roll(pltpu.roll(hl[e], 1, 1), 2, 0)
                total = total + jnp.where((sub8 < 2) & (lane8 == 0), moved * leads, 0.0)
            if q == 3:
                moved = pltpu.roll(pltpu.roll(hr[e], 127, 1), 6, 0)
                total = total + jnp.where((sub8 >= 6) & (lane8 == 127), moved * follows, 0.0)
            flow_o[e, part, :] = total
        return carry

    lax.fori_loop(0, 5, finish, 0)
    for c in sent_a + sent_v + sent_g + sent_h:
        c.wait_send()

    def arrive(n, carry):
        src = lax.rem(space + n, TILES)
        pltpu.make_async_copy(mb, bbuf.at[src], brecv.at[src]).wait()
        return carry

    lax.fori_loop(1, TILES, arrive, 0)
    rr[...] = jnp.zeros_like(rr)
    for cc in range(NC):
        total = bbuf[cc]
        for n in range(1, CHIPS):
            total = total + bbuf[n * NC + cc]
        rr[pl.ds(cc, 1), pl.ds(0, 128)] = total[0:1]
        rr[pl.ds(cc, 1), pl.ds(128, 128)] = total[1:2]
    both = rr[:, pl.ds(0, MODES)]
    columns = lax.dot_general(inv_t[...], both, across, precision=HIGHEST, preferred_element_type=F32)
    modal = jnp.dot(both, inv[...], precision=HIGHEST, preferred_element_type=F32)
    modal_o[...] = modal[0:2]
    for s in range(2):
        coef[s] = jnp.broadcast_to(columns[:, s : s + 1], (MODES, 128))

    def expand(n, carry):
        d = n // (CT // EJ)
        j0 = lax.rem(n, CT // EJ) * EJ
        sums = [[jnp.zeros((8, 128), F32) for _ in range(EJ)] for _ in range(2)]
        for g in range(GROUPS):
            c0, c1 = coef[0, pl.ds(8 * g, 8), :], coef[1, pl.ds(8 * g, 8), :]
            for i in range(EJ):
                tile = shp[d, pl.ds(8 * g, 8), pl.ds(pl.multiple_of((j0 + i) * 128, 128), 128)]
                sums[0][i] = sums[0][i] + c0 * tile
                sums[1][i] = sums[1][i] + c1 * tile
        for i in range(EJ):
            for s in range(2):
                row = 2 * (j0 + i) + s
                line = jnp.sum(sums[s][i], axis=0, keepdims=True)
                mesh_o[d, pl.ds(row, 1), :] = line * surf2[pl.ds(row, 1), :]
        return carry

    lax.fori_loop(0, 3 * (CT // EJ), expand, 0)

    def drain(n, carry):
        pltpu.make_async_copy(mb, mb, bsend.at[n]).wait()
        return carry

    lax.fori_loop(0, TILES - 1, drain, 0)


def place(*refs):
    copies = [pltpu.make_async_copy(refs[i], refs[3 + i], refs[6].at[i]) for i in range(3)]
    for copy in copies:
        copy.start()
    for copy in copies:
        copy.wait()


def shards(
    adjoint, jac_cell, jac_left, jac_right, volume, normals, surface, instance_map, mode_shapes, damping, modal_inverse
):
    def tiles(array):
        lead = array.shape[1:-1]
        n = len(lead)
        split = array.reshape((2,) + lead + (CT, 128))
        order = tuple(range(1, n + 1)) + (n + 1, 0, n + 2)
        return split.transpose(order).reshape(lead + (2 * CT, 128))

    def slots(array):
        lead = array.shape[0]
        return array.reshape(lead, CT, 2, 128).transpose(2, 0, 1, 3).reshape(2, lead, CT * 128)

    args = (
        tiles(adjoint),
        tiles(jac_cell),
        tiles(jac_left),
        tiles(jac_right),
        volume.reshape(CT, 128),
        normals,
        surface.reshape(CT, 128),
        instance_map.reshape(1, 8),
        mode_shapes.transpose(1, 0, 2),
        damping.reshape(1, MODES),
        modal_inverse,
    )
    vmem = pltpu.VMEM
    results = ((5, 2 * CT, 128), (3, 2 * CT, 128), (2, MODES))
    dma = pltpu.SemaphoreType.DMA
    flow, mesh, modal = pl.pallas_call(
        kernel,
        out_shape=tuple(vmem(shape, F32) for shape in results),
        in_specs=[pl.BlockSpec(memory_space=pl.ANY)] * len(args),
        out_specs=[pl.BlockSpec(memory_space=pltpu.VMEM)] * 3,
        scratch_shapes=[
            vmem((NY, 5, 32, 128), F32),
            vmem((3, 5, 32, 128), F32),
            vmem((3, 5, 4, 32, 128), F32),
            vmem((CT, 128), F32),
            vmem((3, CT * 128), F32),
            vmem((CT, 128), jnp.int32),
            vmem((1, 8), jnp.int32),
            vmem((3, MODES, CT * 128), F32),
            vmem((1, MODES), F32),
            vmem((MODES, MODES), F32),
            vmem((2, 32, 128), F32),
            vmem((32, 128), F32),
            vmem((32, 128), F32),
            vmem((3, CT, 128), F32),
            vmem((4, 3 * CT, 128), F32),
            vmem((6, ROWS, 128), F32),
            vmem((5, 32, 128), F32),
            vmem((5, 32, 128), F32),
            vmem((5, 32, 128), F32),
            vmem((8, 8), F32),
            vmem((4, WIDE), F32),
            vmem((NY * NC, 4, WIDE), F32),
            vmem((2, WIDE), F32),
            vmem((4, 2, WIDE), F32),
            vmem((2, 8, WIDE), F32),
            vmem((2, 8, WIDE), F32),
            vmem((2, 128), F32),
            vmem((TILES, 2, 128), F32),
            vmem((8, WIDE), F32),
            vmem((MODES, MODES), F32),
            vmem((2, MODES, 128), F32),
            vmem((5, 8, 128), F32),
            vmem((5, 8, 128), F32),
            dma((13,)),
            dma((CHUNKS,)),
            pltpu.SemaphoreType.REGULAR,
            dma((NY * NC,)),
            dma((NY * NC,)),
            dma((3,)),
            dma((4,)),
            dma((2,)),
            dma((2,)),
            dma((NY,)),
            dma((NY,)),
            dma((TILES,)),
            dma((TILES,)),
        ],
        compiler_params=pltpu.CompilerParams(
            collective_id=0, has_side_effects=True, vmem_limit_bytes=56 * 1024 * 1024
        ),
    )(*args)
    flow, mesh, modal = pl.pallas_call(
        place,
        out_shape=tuple(jax.ShapeDtypeStruct(shape, F32) for shape in results),
        in_specs=[pl.BlockSpec(memory_space=pltpu.VMEM)] * 3,
        out_specs=[pl.BlockSpec(memory_space=pltpu.HBM)] * 3,
        scratch_shapes=[dma((3,))],
    )(*(pltpu.with_memory_space_constraint(part, pltpu.VMEM) for part in (flow, mesh, modal)))
    return slots(flow), slots(mesh), modal


def solution(mesh):
    placed = (
        P("inst", None, "space"),
        P("inst", None, None, "space"),
        P("inst", None, None, "space"),
        P("inst", None, None, "space"),
        P("space"),
        P(None, "space"),
        P("space"),
        P(),
        P(None, None, "space"),
        P(),
        P(),
    )
    return jax.shard_map(
        shards,
        mesh=mesh,
        in_specs=placed,
        out_specs=(P("inst", None, "space"), P("inst", None, "space"), P("inst", None)),
        check_vma=False,
    )
```

```python
import jax
import jax.numpy as jnp
from jax import lax
from jax.experimental import pallas as pl
from jax.experimental.pallas import tpu as pltpu
from jax.sharding import PartitionSpec as P

MESH = pl.DeviceIdType.MESH
HIGHEST = lax.Precision.HIGHEST
F32 = jnp.float32

NZ, NX, NY, NC = 8, 4, 4, 2
TILES = NZ * NX * NC
CHIPS = NZ * NX
MODES = 200
ROWS = 208
WIDE = 256
CT = 16
CELLS = CT * 128
CHUNKS = 8
CW = CELLS // CHUNKS
EW = 512
BF16 = jnp.bfloat16


def halves(value):
    upper = value.astype(BF16).astype(F32)
    return jnp.concatenate([upper, value - upper], axis=0).astype(BF16)


def iota(shape, dim):
    return lax.broadcasted_iota(jnp.int32, shape, dim)


def next_cell(x):
    shape = x.shape
    rolled = pltpu.roll(x, 127, 1)
    carried = pltpu.roll(rolled, shape[0] - 2, 0)
    carried = jnp.where(iota(shape, 0) >= shape[0] - 2, 0.0, carried)
    return jnp.where(iota(shape, 1) == 127, carried, rolled)


def previous_cell(x):
    shape = x.shape
    rolled = pltpu.roll(x, 1, 1)
    carried = pltpu.roll(rolled, 2, 0)
    carried = jnp.where(iota(shape, 0) < 2, 0.0, carried)
    return jnp.where(iota(shape, 1) == 0, carried, rolled)


def coupling_of(differ):
    d = differ.astype(F32)
    angle = d * (jnp.pi / 8)
    same = differ == 0
    sine = jnp.where(same, 1.0, jnp.sin(angle))
    return jnp.where(same, 0.0, 0.5 * jnp.cos(jnp.pi * d) * jnp.cos(angle) / sine)


def kernel(
    adj_h, adjw_h, jc_h, jl_h, jr_h, jcw_h, jlw_h, jrw_h, vol_h, volw_h, nrm_h, surf_h, imap_h, shp_h, damp_h, inv_h,
    flow_o, mesh_o, modal_o,
    adj, adjw, jac4, jac, vol, volw, nrm, surf, imap, shp, damp, inv,
    vol2, wf, w16, shi, slo, fl, fr, fb,
    ma, abuf, vmsg, vbuf, xl, xp, mb, bbuf, rr, mm,
    hl, hr,
    lsem, csem, ready,
    asend, arecv, vsend, vrecv, hsend, hrecv, gsend, grecv, bsend, brecv,
):
    space, y = lax.axis_index("space"), lax.axis_index("inst")
    core = lax.rem(space, NC)
    chip = space // NC
    x = lax.rem(chip, NX)
    z = chip // NX
    other = 1 - core

    def at(zz, xx, cc):
        return (zz * NX + xx) * NC + cc

    def bring(src, dst, sem):
        copy = pltpu.make_async_copy(src, dst, sem)
        copy.start()
        return copy

    c_first = [bring(adjw_h, adjw, lsem.at[0])]
    c_first += [bring(j.at[:, 4], jac4.at[i], lsem.at[1 + i]) for i, j in enumerate((jcw_h, jlw_h, jrw_h))]
    c_first += [bring(volw_h, volw, lsem.at[4]), bring(surf_h, surf, lsem.at[5]), bring(nrm_h, nrm, lsem.at[6])]

    def chunk(k):
        part = pl.ds(pl.multiple_of(k * CW, CW), CW)
        return pltpu.make_async_copy(shp_h.at[:, :, part], shp.at[:, pl.ds(0, MODES), part], csem.at[k])

    for k in range(CHUNKS):
        chunk(k).start()

    barrier = pltpu.get_barrier_semaphore()

    def greet(where, inst):
        pl.semaphore_signal(barrier, inc=1, device_id=(where, inst), device_id_type=MESH)

    for dy in range(1, NY):
        for cc in range(NC):
            greet(at(z, x, cc), lax.rem(y + dy, NY))
    for dx in range(1, NX):
        for cc in range(NC):
            greet(at(z, lax.rem(x + dx, NX), cc), y)
    for dz in range(1, NZ):
        for cc in range(NC):
            greet(at(lax.rem(z + dz, NZ), x, cc), y)
    greet(at(z, x, other), y)
    greet(lax.rem(chip + CHIPS - 1, CHIPS) * NC + 1, y)
    greet(lax.rem(chip + 1, CHIPS) * NC, y)
    greeted = (NY - 1) * NC + (NX - 1) * NC + (NZ - 1) * NC + 3

    ma[...] = jnp.zeros_like(ma)
    vmsg[...] = jnp.zeros_like(vmsg)
    wf[...] = jnp.zeros_like(wf)
    for d in range(3):
        shp[d, pl.ds(MODES, ROWS - MODES), :] = jnp.zeros((ROWS - MODES, CELLS), F32)

    for c in c_first:
        c.wait()

    def direct4(i):
        total = jac4[i, 0] * adjw[0]
        for f in range(1, 5):
            total = total + jac4[i, f] * adjw[f]
        return total

    left4, right4 = direct4(1), direct4(2)
    cell = iota((2, CELLS), 1)
    base4 = direct4(0) + jnp.where(cell == CELLS - 1, 0.0, pltpu.roll(left4, CELLS - 1, 1))
    base4 = base4 + jnp.where(cell == 0, 0.0, pltpu.roll(right4, 1, 1))
    late4 = volw[...] * adjw[4]
    walls = surf[...].astype(F32)
    for d in range(3):
        part = pl.ds(d * CELLS, CELLS)
        g = nrm[pl.ds(d, 1), :] * walls
        wf[pl.ds(0, 2), part] = base4 * g
        wf[pl.ds(2, 2), part] = late4 * g
        wf[pl.ds(4, 1), pl.ds(d * CELLS, 128)] = jnp.where(iota((1, 128), 1) == 0, g[:, 0:128], 0.0)
        wf[pl.ds(5, 1), pl.ds((d + 1) * CELLS - 128, 128)] = jnp.where(iota((1, 128), 1) == 127, g[:, CELLS - 128 :], 0.0)
    w16[...] = halves(wf[...])

    across = (((1,), (1,)), ((), ()))

    def project(k, carry):
        chunk(k).wait()
        high, low = carry
        for d in range(3):
            part = pl.ds(pl.multiple_of(k * CW, CW), CW)
            tile = shp[d, :, part]
            upper = tile.astype(BF16)
            lower = (tile - upper.astype(F32)).astype(BF16)
            shi[d, :, part] = upper
            slo[d, :, part] = lower
            weight = w16[:, pl.ds(pl.multiple_of(d * CELLS + k * CW, CW), CW)]
            high = high + lax.dot_general(weight, upper, across, preferred_element_type=F32)
            low = low + lax.dot_general(weight, lower, across, preferred_element_type=F32)
        return high, low

    nothing = jnp.zeros((16, ROWS), F32)
    high, low = lax.fori_loop(0, CHUNKS, project, (nothing, nothing))
    both = high + low
    summed = both[0:8] + both[8:16]
    ma[:, pl.ds(0, ROWS)] = summed[0:4]
    vmsg[:, pl.ds(0, ROWS)] = summed[4:6]
    lanes = iota((2, 128), 1)
    tail = ma[pl.ds(0, 2), pl.ds(128, 128)]
    tail = jnp.where(lanes == MODES - 128, left4[:, 0:1], tail)
    tail = jnp.where(lanes == MODES + 1 - 128, right4[:, CELLS - 1 :], tail)
    ma[pl.ds(0, 2), pl.ds(128, 128)] = tail

    c_imap = bring(imap_h, imap, lsem.at[7])
    c_damp = bring(damp_h, damp, lsem.at[8])
    c_inv = bring(inv_h, inv, lsem.at[9])
    c_jac = [bring(j, jac.at[i], lsem.at[10 + i]) for i, j in enumerate((jc_h, jl_h, jr_h))]
    c_jac += [bring(adj_h, adj.at[y], lsem.at[13]), bring(vol_h, vol, lsem.at[14])]
    pl.semaphore_wait(barrier, greeted)
    for dx in range(1, NX):
        for cc in range(NC):
            pl.semaphore_signal(ready, inc=1, device_id=(at(z, lax.rem(x + dx, NX), cc), y), device_id_type=MESH)

    def send(src, dst, ssem, rsem, where, inst):
        copy = pltpu.make_async_remote_copy(
            src_ref=src, dst_ref=dst, send_sem=ssem, recv_sem=rsem, device_id=(where, inst), device_id_type=MESH
        )
        copy.start()
        return copy

    mine = y * NC + core
    sent_a = []
    for dy, dc in ((2, 0), (2, 1), (1, 0), (3, 0), (1, 1), (3, 1), (0, 1)):
        n = dy * NC + dc
        cc = lax.rem(core + dc, NC)
        sent_a.append(send(ma, abuf.at[mine], asend.at[n], arecv.at[mine], at(z, x, cc), lax.rem(y + dy, NY)))
    sent_v = [send(vmsg, vbuf.at[core], vsend.at[0], vrecv.at[core], at(z, x, other), y)]
    outer = lax.rem(chip + 2 * core - 1 + CHIPS, CHIPS)
    slot = 3 - core
    for cc in range(NC):
        sent_v.append(send(vmsg, vbuf.at[slot], vsend.at[1 + cc], vrecv.at[slot], outer * NC + cc, y))
    abuf[pl.ds(mine, 1)] = ma[...][None]
    vbuf[pl.ds(core, 1)] = vmsg[...][None]

    for c in c_jac:
        c.wait()
    for s in range(2):
        vol2[pl.ds(s, CT, stride=2), :] = vol[...]
    sent_g = []
    for dy in range(1, NY):
        sent_g.append(send(adj.at[y], adj.at[y], gsend.at[dy], grecv.at[y], space, lax.rem(y + dy, NY)))

    def combine(j, e):
        total = j[0, e] * adj[y, 0]
        for f in range(1, 5):
            total = total + j[f, e] * adj[y, f]
        return total

    def component(e, carry):
        left, right = combine(jac.at[1], e), combine(jac.at[2], e)
        fl[e] = left
        fr[e] = right
        fb[e] = combine(jac.at[0], e) + next_cell(left) + previous_cell(right)
        return carry

    lax.fori_loop(0, 5, component, 0)
    before, after = lax.rem(space + TILES - 1, TILES), lax.rem(space + 1, TILES)
    sent_h = [
        send(fl.at[:, pl.ds(0, 8), :], hr, hsend.at[0], hrecv.at[0], before, y),
        send(fr.at[:, pl.ds(24, 8), :], hl, hsend.at[1], hrecv.at[1], after, y),
    ]

    c_imap.wait()
    c_damp.wait()
    c_inv.wait()
    eight = iota((8, 8), 0) == iota((8, 8), 1)
    slots = jnp.broadcast_to(imap[...], (8, 8))
    down = jnp.sum(jnp.where(eight, slots.astype(F32), 0.0), axis=1, keepdims=True)
    differ = jnp.broadcast_to(down, (8, 8)) - slots.astype(F32)
    h = coupling_of(differ.astype(jnp.int32))
    own = 2 * y + core
    lanes8 = iota((8, 8), 1)
    own_h = jnp.sum(jnp.where(lanes8 == own, h, 0.0), axis=1, keepdims=True)

    for n in range(1, NY * NC):
        dy, dc = n // NC, n % NC
        src = lax.rem(y + dy, NY) * NC + lax.rem(core + dc, NC)
        pltpu.make_async_copy(ma, abuf.at[src], arecv.at[src]).wait()
    pltpu.make_async_copy(vmsg, vbuf.at[other], vrecv.at[other]).wait()
    for v in (2, 3):
        pltpu.make_async_copy(vmsg, vbuf.at[v], vrecv.at[v]).wait()
    for cc in range(NC):
        for yy in range(NY):
            xl[cc, pl.ds(2 * yy, 2), :] = abuf[yy * NC + cc, pl.ds(0, 2), :]
            xp[cc, pl.ds(2 * yy, 2), :] = abuf[yy * NC + cc, pl.ds(2, 2), :]
    has_before = jnp.where(chip > 0, 1.0, 0.0)
    has_after = jnp.where(chip < CHIPS - 1, 1.0, 0.0)
    proj = xl[0] + xl[1]
    edges = (
        (xl[0][:, 200:201] * has_before, vbuf[2, pl.ds(1, 1), :]),
        (xl[0][:, 201:202], vbuf[1, pl.ds(0, 1), :]),
        (xl[1][:, 200:201], vbuf[0, pl.ds(1, 1), :]),
        (xl[1][:, 201:202] * has_after, vbuf[3, pl.ds(0, 1), :]),
    )
    for amount, vector in edges:
        proj = proj + amount * vector
    late = xp[0] + xp[1]
    for a in range(8):
        proj = proj - h[:, a : a + 1] * late[a : a + 1, :]
    plain = jnp.sum(jnp.where(iota((8, WIDE), 0) == own, proj, 0.0), axis=0, keepdims=True)
    mixed = jnp.sum(own_h * proj, axis=0, keepdims=True)
    rhs = plain[:, 0:MODES] + damp[...] * mixed[:, 0:MODES]
    mb[...] = jnp.zeros_like(mb)
    mb[pl.ds(0, 1), :] = rhs[:, 0:128]
    mb[pl.ds(1, 1), pl.ds(0, MODES - 128)] = rhs[:, 128:MODES]

    pl.semaphore_wait(ready, (NX - 1) * NC)

    def hops(offset):
        dz, dx, _ = offset
        return min(dz, NZ - dz) + min(dx, NX - dx)

    offsets = [(dz, dx, dc) for dz in range(NZ) for dx in range(NX) for dc in range(NC)][1:]
    for n, (dz, dx, dc) in enumerate(sorted(offsets, key=hops, reverse=True)):
        where = at(lax.rem(z + dz, NZ), lax.rem(x + dx, NX), lax.rem(core + dc, NC))
        send(mb, bbuf.at[space], bsend.at[n], brecv.at[space], where, y)

    rr[...] = jnp.zeros_like(rr)
    mm[...] = jnp.zeros_like(mm)
    pltpu.make_async_copy(hr, hr, hrecv.at[0]).wait()
    pltpu.make_async_copy(hl, hl, hrecv.at[1]).wait()
    for dy in range(1, NY):
        src = lax.rem(y + dy, NY)
        pltpu.make_async_copy(adj.at[src], adj.at[src], grecv.at[src]).wait()
    lane8, sub8 = iota((8, 128), 1), iota((8, 128), 0)
    parity = lax.rem(sub8, 2)
    pick = [jnp.sum(jnp.where(lanes8 == 2 * y + s, h, 0.0), axis=1, keepdims=True) for s in range(2)]

    def entry(a, s):
        return jnp.broadcast_to(pick[s][a : a + 1, :], (8, 128))

    same = [jnp.where(parity == 0, entry(2 * yy, 0), entry(2 * yy + 1, 1)) for yy in range(NY)]
    cross = [jnp.where(parity == 0, entry(2 * yy + 1, 0), entry(2 * yy, 1)) for yy in range(NY)]
    follows = jnp.where(space < TILES - 1, 1.0, 0.0)
    leads = jnp.where(space > 0, 1.0, 0.0)

    def finish(e, carry):
        for q in range(4):
            part = pl.ds(8 * q, 8)
            timed = jnp.zeros((8, 128), F32)
            for yy in range(NY):
                here = adj[yy, e, part, :]
                swapped = jnp.where(parity == 0, pltpu.roll(here, 7, 0), pltpu.roll(here, 1, 0))
                timed = timed + here * same[yy] + swapped * cross[yy]
            total = fb[e, part, :] + vol2[part, :] * timed
            if q == 0:
                moved = pltpu.roll(pltpu.roll(hl[e], 1, 1), 2, 0)
                total = total + jnp.where((sub8 < 2) & (lane8 == 0), moved * leads, 0.0)
            if q == 3:
                moved = pltpu.roll(pltpu.roll(hr[e], 127, 1), 6, 0)
                total = total + jnp.where((sub8 >= 6) & (lane8 == 127), moved * follows, 0.0)
            flow_o[e, part, :] = total
        return carry

    lax.fori_loop(0, 5, finish, 0)
    for c in sent_a + sent_v + sent_g + sent_h:
        c.wait_send()

    own_sum, other_sum = mb[...], jnp.zeros((2, 128), F32)
    for dz, dx, dc in sorted(offsets, key=hops):
        src = at(lax.rem(z + dz, NZ), lax.rem(x + dx, NX), lax.rem(core + dc, NC))
        pltpu.make_async_copy(mb, bbuf.at[src], brecv.at[src]).wait()
        if dc == 0:
            own_sum = own_sum + bbuf[src]
        else:
            other_sum = other_sum + bbuf[src]
    even = jnp.broadcast_to(core, (2, 128)) == 0
    for row, total in enumerate((jnp.where(even, own_sum, other_sum), jnp.where(even, other_sum, own_sum))):
        rr[pl.ds(row, 1), pl.ds(0, 128)] = total[0:1]
        rr[pl.ds(row, 1), pl.ds(128, 128)] = total[1:2]
    modal = jnp.dot(rr[:, pl.ds(0, MODES)], inv[...], precision=HIGHEST, preferred_element_type=F32)
    modal_o[...] = modal[0:2]
    mm[:, pl.ds(0, MODES)] = modal
    lead = halves(mm[:, pl.ds(0, ROWS)])
    plain_dot = (((1,), (0,)), ((), ()))
    for d in range(3):
        for k in range(CELLS // EW):
            part = pl.ds(k * EW, EW)
            spread = lax.dot_general(lead, shi[d, :, part], plain_dot, preferred_element_type=F32)
            spread = spread + lax.dot_general(lead, slo[d, :, part], plain_dot, preferred_element_type=F32)
            mesh_o[d, :, part] = (spread[0:8] + spread[8:16])[0:2] * surf[:, part].astype(F32)

    def drain(n, carry):
        pltpu.make_async_copy(mb, mb, bsend.at[n]).wait()
        return carry

    lax.fori_loop(0, TILES - 1, drain, 0)


def place(*refs):
    copies = [pltpu.make_async_copy(refs[i], refs[3 + i], refs[6].at[i]) for i in range(3)]
    for copy in copies:
        copy.start()
    for copy in copies:
        copy.wait()


def shards(
    adjoint, jac_cell, jac_left, jac_right, volume, normals, surface, instance_map, mode_shapes, damping, modal_inverse
):
    def tiles(array):
        lead = array.shape[1:-1]
        n = len(lead)
        split = array.reshape((2,) + lead + (CT, 128))
        order = tuple(range(1, n + 1)) + (n + 1, 0, n + 2)
        return split.transpose(order).reshape(lead + (2 * CT, 128))

    def slots(array):
        lead = array.shape[0]
        return array.reshape(lead, CT, 2, 128).transpose(2, 0, 1, 3).reshape(2, lead, CT * 128)

    def wide(array):
        return jnp.moveaxis(array, 0, -2)

    args = (
        tiles(adjoint),
        wide(adjoint),
        tiles(jac_cell),
        tiles(jac_left),
        tiles(jac_right),
        wide(jac_cell),
        wide(jac_left),
        wide(jac_right),
        volume.reshape(CT, 128),
        volume.reshape(1, CELLS),
        normals,
        surface.reshape(1, CELLS),
        instance_map.reshape(1, 8),
        mode_shapes.transpose(1, 0, 2),
        damping.reshape(1, MODES),
        modal_inverse,
    )
    vmem = pltpu.VMEM
    results = ((5, 2 * CT, 128), (3, 2, CELLS), (2, MODES))
    dma = pltpu.SemaphoreType.DMA
    flow, mesh, modal = pl.pallas_call(
        kernel,
        out_shape=tuple(vmem(shape, F32) for shape in results),
        in_specs=[pl.BlockSpec(memory_space=pl.ANY)] * len(args),
        out_specs=[pl.BlockSpec(memory_space=pltpu.VMEM)] * 3,
        scratch_shapes=[
            vmem((NY, 5, 32, 128), F32),
            vmem((5, 2, CELLS), F32),
            vmem((3, 5, 2, CELLS), F32),
            vmem((3, 5, 5, 32, 128), F32),
            vmem((CT, 128), F32),
            vmem((1, CELLS), F32),
            vmem((3, CELLS), F32),
            vmem((1, CELLS), jnp.int32),
            vmem((1, 8), jnp.int32),
            vmem((3, ROWS, CELLS), F32),
            vmem((1, MODES), F32),
            vmem((MODES, MODES), F32),
            vmem((32, 128), F32),
            vmem((8, 3 * CELLS), F32),
            vmem((16, 3 * CELLS), BF16),
            vmem((3, ROWS, CELLS), BF16),
            vmem((3, ROWS, CELLS), BF16),
            vmem((5, 32, 128), F32),
            vmem((5, 32, 128), F32),
            vmem((5, 32, 128), F32),
            vmem((4, WIDE), F32),
            vmem((NY * NC, 4, WIDE), F32),
            vmem((2, WIDE), F32),
            vmem((4, 2, WIDE), F32),
            vmem((2, 8, WIDE), F32),
            vmem((2, 8, WIDE), F32),
            vmem((2, 128), F32),
            vmem((TILES, 2, 128), F32),
            vmem((8, WIDE), F32),
            vmem((8, WIDE), F32),
            vmem((5, 8, 128), F32),
            vmem((5, 8, 128), F32),
            dma((15,)),
            dma((CHUNKS,)),
            pltpu.SemaphoreType.REGULAR,
            dma((NY * NC,)),
            dma((NY * NC,)),
            dma((3,)),
            dma((4,)),
            dma((2,)),
            dma((2,)),
            dma((NY,)),
            dma((NY,)),
            dma((TILES,)),
            dma((TILES,)),
        ],
        compiler_params=pltpu.CompilerParams(
            collective_id=0, has_side_effects=True, vmem_limit_bytes=56 * 1024 * 1024
        ),
    )(*args)
    flow, mesh, modal = pl.pallas_call(
        place,
        out_shape=tuple(jax.ShapeDtypeStruct(shape, F32) for shape in results),
        in_specs=[pl.BlockSpec(memory_space=pltpu.VMEM)] * 3,
        out_specs=[pl.BlockSpec(memory_space=pltpu.HBM)] * 3,
        scratch_shapes=[dma((3,))],
    )(*(pltpu.with_memory_space_constraint(part, pltpu.VMEM) for part in (flow, mesh, modal)))
    return slots(flow), mesh.transpose(1, 0, 2), modal


def solution(mesh):
    placed = (
        P("inst", None, "space"),
        P("inst", None, None, "space"),
        P("inst", None, None, "space"),
        P("inst", None, None, "space"),
        P("space"),
        P(None, "space"),
        P("space"),
        P(),
        P(None, None, "space"),
        P(),
        P(),
    )
    return jax.shard_map(
        shards,
        mesh=mesh,
        in_specs=placed,
        out_specs=(P("inst", None, "space"), P("inst", None, "space"), P("inst", None)),
        check_vma=False,
    )
```

```python
import jax
import jax.numpy as jnp
from jax import lax
from jax.experimental import pallas as pl
from jax.experimental.pallas import tpu as pltpu
from jax.sharding import PartitionSpec as P

MESH = pl.DeviceIdType.MESH
HIGHEST = lax.Precision.HIGHEST
F32 = jnp.float32

NZ, NX, NY, NC = 8, 4, 4, 2
TILES = NZ * NX * NC
CHIPS = NZ * NX
MODES = 200
ROWS = 208
WIDE = 256
CT = 16
CELLS = CT * 128
CHUNKS = 4
AHEAD = 4
CW = CELLS // CHUNKS
EW = 512
BF16 = jnp.bfloat16


def halves(value):
    upper = value.astype(BF16).astype(F32)
    return jnp.concatenate([upper, value - upper], axis=0).astype(BF16)


def iota(shape, dim):
    return lax.broadcasted_iota(jnp.int32, shape, dim)


def next_cell(x):
    shape = x.shape
    rolled = pltpu.roll(x, 127, 1)
    carried = pltpu.roll(rolled, shape[0] - 2, 0)
    carried = jnp.where(iota(shape, 0) >= shape[0] - 2, 0.0, carried)
    return jnp.where(iota(shape, 1) == 127, carried, rolled)


def previous_cell(x):
    shape = x.shape
    rolled = pltpu.roll(x, 1, 1)
    carried = pltpu.roll(rolled, 2, 0)
    carried = jnp.where(iota(shape, 0) < 2, 0.0, carried)
    return jnp.where(iota(shape, 1) == 0, carried, rolled)


def coupling_of(differ):
    d = differ.astype(F32)
    angle = d * (jnp.pi / 8)
    same = differ == 0
    sine = jnp.where(same, 1.0, jnp.sin(angle))
    return jnp.where(same, 0.0, 0.5 * jnp.cos(jnp.pi * d) * jnp.cos(angle) / sine)


def kernel(
    adj_h, adjw_h, jc_h, jl_h, jr_h, jcw_h, jlw_h, jrw_h, vol_h, volw_h, nrm_h, surf_h, imap_h, shp_h, damp_h, inv_h,
    flow_o, mesh_o, modal_o,
    adj, adjw, jac4, jac, vol, volw, nrm, surf, imap, shp, damp, inv,
    vol2, wf, w16, shi, slo, fl, fr, fb,
    ma, abuf, vmsg, vbuf, xl, xp, mb, bbuf, rr, mm,
    hl, hr,
    lsem, csem, ready,
    asend, arecv, vsend, vrecv, hsend, hrecv, gsend, grecv, bsend, brecv,
):
    space, y = lax.axis_index("space"), lax.axis_index("inst")
    core = lax.rem(space, NC)
    chip = space // NC
    x = lax.rem(chip, NX)
    z = chip // NX
    other = 1 - core

    def at(zz, xx, cc):
        return (zz * NX + xx) * NC + cc

    def bring(src, dst, sem):
        copy = pltpu.make_async_copy(src, dst, sem)
        copy.start()
        return copy

    c_first = [bring(adjw_h, adjw, lsem.at[0])]
    c_first += [bring(j.at[:, 4], jac4.at[i], lsem.at[1 + i]) for i, j in enumerate((jcw_h, jlw_h, jrw_h))]
    c_first += [bring(volw_h, volw, lsem.at[4]), bring(surf_h, surf, lsem.at[5]), bring(nrm_h, nrm, lsem.at[6])]

    def chunk(k):
        part = pl.ds(pl.multiple_of(k * CW, CW), CW)
        return pltpu.make_async_copy(shp_h.at[:, :, part], shp.at[:, pl.ds(0, MODES), part], csem.at[k])

    for k in range(AHEAD):
        chunk(k).start()

    barrier = pltpu.get_barrier_semaphore()

    def greet(where, inst):
        pl.semaphore_signal(barrier, inc=1, device_id=(where, inst), device_id_type=MESH)

    for dy in range(1, NY):
        for cc in range(NC):
            greet(at(z, x, cc), lax.rem(y + dy, NY))
    for dx in range(1, NX):
        greet(at(z, lax.rem(x + dx, NX), core), y)
    for dz in range(1, NZ):
        greet(at(lax.rem(z + dz, NZ), x, core), y)
    greet(at(z, x, other), y)
    greet(lax.rem(chip + CHIPS - 1, CHIPS) * NC + 1, y)
    greet(lax.rem(chip + 1, CHIPS) * NC, y)
    greeted = (NY - 1) * NC + (NX - 1) + (NZ - 1) + 3

    ma[...] = jnp.zeros_like(ma)
    vmsg[...] = jnp.zeros_like(vmsg)
    wf[...] = jnp.zeros_like(wf)
    for d in range(3):
        shp[d, pl.ds(MODES, ROWS - MODES), :] = jnp.zeros((ROWS - MODES, CELLS), F32)

    for c in c_first:
        c.wait()

    def direct4(i):
        total = jac4[i, 0] * adjw[0]
        for f in range(1, 5):
            total = total + jac4[i, f] * adjw[f]
        return total

    left4, right4 = direct4(1), direct4(2)
    cell = iota((2, CELLS), 1)
    base4 = direct4(0) + jnp.where(cell == CELLS - 1, 0.0, pltpu.roll(left4, CELLS - 1, 1))
    base4 = base4 + jnp.where(cell == 0, 0.0, pltpu.roll(right4, 1, 1))
    late4 = volw[...] * adjw[4]
    walls = surf[...].astype(F32)
    for d in range(3):
        part = pl.ds(d * CELLS, CELLS)
        g = nrm[pl.ds(d, 1), :] * walls
        wf[pl.ds(0, 2), part] = base4 * g
        wf[pl.ds(2, 2), part] = late4 * g
        wf[pl.ds(4, 1), pl.ds(d * CELLS, 128)] = jnp.where(iota((1, 128), 1) == 0, g[:, 0:128], 0.0)
        wf[pl.ds(5, 1), pl.ds((d + 1) * CELLS - 128, 128)] = jnp.where(iota((1, 128), 1) == 127, g[:, CELLS - 128 :], 0.0)
    w16[...] = halves(wf[...])

    across = (((1,), (1,)), ((), ()))

    def project(k, carry):
        chunk(k).wait()
        if AHEAD < CHUNKS:

            @pl.when(k + AHEAD < CHUNKS)
            def _():
                chunk(k + AHEAD).start()

        high, low = carry
        for d in range(3):
            part = pl.ds(pl.multiple_of(k * CW, CW), CW)
            tile = shp[d, :, part]
            upper = tile.astype(BF16)
            lower = (tile - upper.astype(F32)).astype(BF16)
            shi[d, :, part] = upper
            slo[d, :, part] = lower
            weight = w16[:, pl.ds(pl.multiple_of(d * CELLS + k * CW, CW), CW)]
            high = high + lax.dot_general(weight, upper, across, preferred_element_type=F32)
            low = low + lax.dot_general(weight, lower, across, preferred_element_type=F32)
        return high, low

    nothing = jnp.zeros((16, ROWS), F32)
    high, low = lax.fori_loop(0, CHUNKS, project, (nothing, nothing))
    both = high + low
    summed = both[0:8] + both[8:16]
    ma[:, pl.ds(0, ROWS)] = summed[0:4]
    vmsg[:, pl.ds(0, ROWS)] = summed[4:6]
    lanes = iota((2, 128), 1)
    tail = ma[pl.ds(0, 2), pl.ds(128, 128)]
    tail = jnp.where(lanes == MODES - 128, left4[:, 0:1], tail)
    tail = jnp.where(lanes == MODES + 1 - 128, right4[:, CELLS - 1 :], tail)
    ma[pl.ds(0, 2), pl.ds(128, 128)] = tail

    c_imap = bring(imap_h, imap, lsem.at[7])
    c_damp = bring(damp_h, damp, lsem.at[8])
    c_inv = bring(inv_h, inv, lsem.at[9])
    c_jac = [bring(j, jac.at[i], lsem.at[10 + i]) for i, j in enumerate((jc_h, jl_h, jr_h))]
    c_jac += [bring(adj_h, adj.at[y], lsem.at[13]), bring(vol_h, vol, lsem.at[14])]
    pl.semaphore_wait(barrier, greeted)
    for dx in range(1, NX):
        pl.semaphore_signal(ready, inc=1, device_id=(at(z, lax.rem(x + dx, NX), core), y), device_id_type=MESH)

    def send(src, dst, ssem, rsem, where, inst):
        copy = pltpu.make_async_remote_copy(
            src_ref=src, dst_ref=dst, send_sem=ssem, recv_sem=rsem, device_id=(where, inst), device_id_type=MESH
        )
        copy.start()
        return copy

    mine = y * NC + core
    sent_a = []
    for dy, dc in ((2, 0), (2, 1), (1, 0), (3, 0), (1, 1), (3, 1), (0, 1)):
        n = dy * NC + dc
        cc = lax.rem(core + dc, NC)
        sent_a.append(send(ma, abuf.at[mine], asend.at[n], arecv.at[mine], at(z, x, cc), lax.rem(y + dy, NY)))
    sent_v = [send(vmsg, vbuf.at[core], vsend.at[0], vrecv.at[core], at(z, x, other), y)]
    outer = lax.rem(chip + 2 * core - 1 + CHIPS, CHIPS)
    slot = 3 - core
    for cc in range(NC):
        sent_v.append(send(vmsg, vbuf.at[slot], vsend.at[1 + cc], vrecv.at[slot], outer * NC + cc, y))
    abuf[pl.ds(mine, 1)] = ma[...][None]
    vbuf[pl.ds(core, 1)] = vmsg[...][None]

    for c in c_jac:
        c.wait()
    for s in range(2):
        vol2[pl.ds(s, CT, stride=2), :] = vol[...]
    sent_g = []
    for dy in range(1, NY):
        sent_g.append(send(adj.at[y], adj.at[y], gsend.at[dy], grecv.at[y], space, lax.rem(y + dy, NY)))

    def combine(j, e):
        total = j[0, e] * adj[y, 0]
        for f in range(1, 5):
            total = total + j[f, e] * adj[y, f]
        return total

    def component(e, carry):
        left, right = combine(jac.at[1], e), combine(jac.at[2], e)
        fl[e] = left
        fr[e] = right
        fb[e] = combine(jac.at[0], e) + next_cell(left) + previous_cell(right)
        return carry

    lax.fori_loop(0, 5, component, 0)
    before, after = lax.rem(space + TILES - 1, TILES), lax.rem(space + 1, TILES)
    sent_h = [
        send(fl.at[:, pl.ds(0, 8), :], hr, hsend.at[0], hrecv.at[0], before, y),
        send(fr.at[:, pl.ds(24, 8), :], hl, hsend.at[1], hrecv.at[1], after, y),
    ]

    c_imap.wait()
    c_damp.wait()
    c_inv.wait()
    eight = iota((8, 8), 0) == iota((8, 8), 1)
    slots = jnp.broadcast_to(imap[...], (8, 8))
    down = jnp.sum(jnp.where(eight, slots.astype(F32), 0.0), axis=1, keepdims=True)
    differ = jnp.broadcast_to(down, (8, 8)) - slots.astype(F32)
    h = coupling_of(differ.astype(jnp.int32))
    lanes8 = iota((8, 8), 1)

    def column_of(s):
        return jnp.sum(jnp.where(lanes8 == 2 * y + s, h, 0.0), axis=1, keepdims=True)

    pick = [column_of(s) for s in range(2)]

    for n in range(1, NY * NC):
        dy, dc = n // NC, n % NC
        src = lax.rem(y + dy, NY) * NC + lax.rem(core + dc, NC)
        pltpu.make_async_copy(ma, abuf.at[src], arecv.at[src]).wait()
    pltpu.make_async_copy(vmsg, vbuf.at[other], vrecv.at[other]).wait()
    for v in (2, 3):
        pltpu.make_async_copy(vmsg, vbuf.at[v], vrecv.at[v]).wait()
    for cc in range(NC):
        for yy in range(NY):
            xl[cc, pl.ds(2 * yy, 2), :] = abuf[yy * NC + cc, pl.ds(0, 2), :]
            xp[cc, pl.ds(2 * yy, 2), :] = abuf[yy * NC + cc, pl.ds(2, 2), :]
    has_before = jnp.where(chip > 0, 1.0, 0.0)
    has_after = jnp.where(chip < CHIPS - 1, 1.0, 0.0)
    proj = xl[0] + xl[1]
    edges = (
        (xl[0][:, 200:201] * has_before, vbuf[2, pl.ds(1, 1), :]),
        (xl[0][:, 201:202], vbuf[1, pl.ds(0, 1), :]),
        (xl[1][:, 200:201], vbuf[0, pl.ds(1, 1), :]),
        (xl[1][:, 201:202] * has_after, vbuf[3, pl.ds(0, 1), :]),
    )
    for amount, vector in edges:
        proj = proj + amount * vector
    late = xp[0] + xp[1]
    for a in range(8):
        proj = proj - h[:, a : a + 1] * late[a : a + 1, :]
    mb[...] = jnp.zeros_like(mb)
    for s in range(2):
        plain = jnp.sum(jnp.where(iota((8, WIDE), 0) == 2 * y + s, proj, 0.0), axis=0, keepdims=True)
        mixed = jnp.sum(pick[s] * proj, axis=0, keepdims=True)
        rhs = plain[:, 0:MODES] + damp[...] * mixed[:, 0:MODES]
        mb[pl.ds(s, 1), :] = rhs[:, 0:128]
        mb[pl.ds(2 + s, 1), pl.ds(0, MODES - 128)] = rhs[:, 128:MODES]

    pl.semaphore_wait(ready, NX - 1)

    def hops(offset):
        dz, dx = offset
        return min(dz, NZ - dz) + min(dx, NX - dx)

    offsets = [(dz, dx) for dz in range(NZ) for dx in range(NX)][1:]
    for n, (dz, dx) in enumerate(sorted(offsets, key=hops, reverse=True)):
        where = at(lax.rem(z + dz, NZ), lax.rem(x + dx, NX), core)
        send(mb, bbuf.at[chip], bsend.at[n], brecv.at[chip], where, y)

    rr[...] = jnp.zeros_like(rr)
    mm[...] = jnp.zeros_like(mm)
    pltpu.make_async_copy(hr, hr, hrecv.at[0]).wait()
    pltpu.make_async_copy(hl, hl, hrecv.at[1]).wait()
    for dy in range(1, NY):
        src = lax.rem(y + dy, NY)
        pltpu.make_async_copy(adj.at[src], adj.at[src], grecv.at[src]).wait()
    lane8, sub8 = iota((8, 128), 1), iota((8, 128), 0)
    parity = lax.rem(sub8, 2)

    def entry(a, s):
        return jnp.broadcast_to(pick[s][a : a + 1, :], (8, 128))

    same = [jnp.where(parity == 0, entry(2 * yy, 0), entry(2 * yy + 1, 1)) for yy in range(NY)]
    cross = [jnp.where(parity == 0, entry(2 * yy + 1, 0), entry(2 * yy, 1)) for yy in range(NY)]
    follows = jnp.where(space < TILES - 1, 1.0, 0.0)
    leads = jnp.where(space > 0, 1.0, 0.0)

    def finish(e, carry):
        for q in range(4):
            part = pl.ds(8 * q, 8)
            timed = jnp.zeros((8, 128), F32)
            for yy in range(NY):
                here = adj[yy, e, part, :]
                swapped = jnp.where(parity == 0, pltpu.roll(here, 7, 0), pltpu.roll(here, 1, 0))
                timed = timed + here * same[yy] + swapped * cross[yy]
            total = fb[e, part, :] + vol2[part, :] * timed
            if q == 0:
                moved = pltpu.roll(pltpu.roll(hl[e], 1, 1), 2, 0)
                total = total + jnp.where((sub8 < 2) & (lane8 == 0), moved * leads, 0.0)
            if q == 3:
                moved = pltpu.roll(pltpu.roll(hr[e], 127, 1), 6, 0)
                total = total + jnp.where((sub8 >= 6) & (lane8 == 127), moved * follows, 0.0)
            flow_o[e, part, :] = total
        return carry

    lax.fori_loop(0, 5, finish, 0)
    for c in sent_a + sent_v + sent_g + sent_h:
        c.wait_send()

    total = mb[...]
    for dz, dx in sorted(offsets, key=hops):
        src = lax.rem(z + dz, NZ) * NX + lax.rem(x + dx, NX)
        pltpu.make_async_copy(mb, bbuf.at[src], brecv.at[src]).wait()
        total = total + bbuf[src]
    rr[pl.ds(0, 2), pl.ds(0, 128)] = total[0:2]
    rr[pl.ds(0, 2), pl.ds(128, 128)] = total[2:4]
    modal = jnp.dot(rr[:, pl.ds(0, MODES)], inv[...], precision=HIGHEST, preferred_element_type=F32)
    modal_o[...] = modal[0:2]
    mm[:, pl.ds(0, MODES)] = modal
    lead = halves(mm[:, pl.ds(0, ROWS)])
    plain_dot = (((1,), (0,)), ((), ()))
    for d in range(3):
        for k in range(CELLS // EW):
            part = pl.ds(k * EW, EW)
            spread = lax.dot_general(lead, shi[d, :, part], plain_dot, preferred_element_type=F32)
            spread = spread + lax.dot_general(lead, slo[d, :, part], plain_dot, preferred_element_type=F32)
            mesh_o[d, :, part] = (spread[0:8] + spread[8:16])[0:2] * surf[:, part].astype(F32)

    def drain(n, carry):
        pltpu.make_async_copy(mb, mb, bsend.at[n]).wait()
        return carry

    lax.fori_loop(0, CHIPS - 1, drain, 0)


def place(*refs):
    copies = [pltpu.make_async_copy(refs[i], refs[3 + i], refs[6].at[i]) for i in range(3)]
    for copy in copies:
        copy.start()
    for copy in copies:
        copy.wait()


def shards(
    adjoint, jac_cell, jac_left, jac_right, volume, normals, surface, instance_map, mode_shapes, damping, modal_inverse
):
    def tiles(array):
        lead = array.shape[1:-1]
        n = len(lead)
        split = array.reshape((2,) + lead + (CT, 128))
        order = tuple(range(1, n + 1)) + (n + 1, 0, n + 2)
        return split.transpose(order).reshape(lead + (2 * CT, 128))

    def slots(array):
        lead = array.shape[0]
        return array.reshape(lead, CT, 2, 128).transpose(2, 0, 1, 3).reshape(2, lead, CT * 128)

    def wide(array):
        return jnp.moveaxis(array, 0, -2)

    args = (
        tiles(adjoint),
        wide(adjoint),
        tiles(jac_cell),
        tiles(jac_left),
        tiles(jac_right),
        wide(jac_cell),
        wide(jac_left),
        wide(jac_right),
        volume.reshape(CT, 128),
        volume.reshape(1, CELLS),
        normals,
        surface.reshape(1, CELLS),
        instance_map.reshape(1, 8),
        mode_shapes.transpose(1, 0, 2),
        damping.reshape(1, MODES),
        modal_inverse,
    )
    vmem = pltpu.VMEM
    results = ((5, 2 * CT, 128), (3, 2, CELLS), (2, MODES))
    dma = pltpu.SemaphoreType.DMA
    flow, mesh, modal = pl.pallas_call(
        kernel,
        out_shape=tuple(vmem(shape, F32) for shape in results),
        in_specs=[pl.BlockSpec(memory_space=pl.ANY)] * len(args),
        out_specs=[pl.BlockSpec(memory_space=pltpu.VMEM)] * 3,
        scratch_shapes=[
            vmem((NY, 5, 32, 128), F32),
            vmem((5, 2, CELLS), F32),
            vmem((3, 5, 2, CELLS), F32),
            vmem((3, 5, 5, 32, 128), F32),
            vmem((CT, 128), F32),
            vmem((1, CELLS), F32),
            vmem((3, CELLS), F32),
            vmem((1, CELLS), jnp.int32),
            vmem((1, 8), jnp.int32),
            vmem((3, ROWS, CELLS), F32),
            vmem((1, MODES), F32),
            vmem((MODES, MODES), F32),
            vmem((32, 128), F32),
            vmem((8, 3 * CELLS), F32),
            vmem((16, 3 * CELLS), BF16),
            vmem((3, ROWS, CELLS), BF16),
            vmem((3, ROWS, CELLS), BF16),
            vmem((5, 32, 128), F32),
            vmem((5, 32, 128), F32),
            vmem((5, 32, 128), F32),
            vmem((4, WIDE), F32),
            vmem((NY * NC, 4, WIDE), F32),
            vmem((2, WIDE), F32),
            vmem((4, 2, WIDE), F32),
            vmem((2, 8, WIDE), F32),
            vmem((2, 8, WIDE), F32),
            vmem((4, 128), F32),
            vmem((CHIPS, 4, 128), F32),
            vmem((8, WIDE), F32),
            vmem((8, WIDE), F32),
            vmem((5, 8, 128), F32),
            vmem((5, 8, 128), F32),
            dma((15,)),
            dma((CHUNKS,)),
            pltpu.SemaphoreType.REGULAR,
            dma((NY * NC,)),
            dma((NY * NC,)),
            dma((3,)),
            dma((4,)),
            dma((2,)),
            dma((2,)),
            dma((NY,)),
            dma((NY,)),
            dma((CHIPS,)),
            dma((CHIPS,)),
        ],
        compiler_params=pltpu.CompilerParams(
            collective_id=0, has_side_effects=True, vmem_limit_bytes=56 * 1024 * 1024
        ),
    )(*args)
    flow, mesh, modal = pl.pallas_call(
        place,
        out_shape=tuple(jax.ShapeDtypeStruct(shape, F32) for shape in results),
        in_specs=[pl.BlockSpec(memory_space=pltpu.VMEM)] * 3,
        out_specs=[pl.BlockSpec(memory_space=pltpu.HBM)] * 3,
        scratch_shapes=[dma((3,))],
    )(*(pltpu.with_memory_space_constraint(part, pltpu.VMEM) for part in (flow, mesh, modal)))
    return slots(flow), mesh.transpose(1, 0, 2), modal


def solution(mesh):
    placed = (
        P("inst", None, "space"),
        P("inst", None, None, "space"),
        P("inst", None, None, "space"),
        P("inst", None, None, "space"),
        P("space"),
        P(None, "space"),
        P("space"),
        P(),
        P(None, None, "space"),
        P(),
        P(),
    )
    return jax.shard_map(
        shards,
        mesh=mesh,
        in_specs=placed,
        out_specs=(P("inst", None, "space"), P("inst", None, "space"), P("inst", None)),
        check_vma=False,
    )
```

```python
import jax
import jax.numpy as jnp
from jax import lax
from jax.experimental import pallas as pl
from jax.experimental.pallas import tpu as pltpu
from jax.sharding import PartitionSpec as P

MESH = pl.DeviceIdType.MESH
HIGHEST = lax.Precision.HIGHEST
F32 = jnp.float32

NZ, NX, NY, NC = 8, 4, 4, 2
TILES = NZ * NX * NC
CHIPS = NZ * NX
MODES = 200
ROWS = 208
WIDE = 256
CT = 16
CELLS = CT * 128
CHUNKS = 4
AHEAD = 4
CW = CELLS // CHUNKS
EW = 512
BF16 = jnp.bfloat16


def halves(value):
    upper = value.astype(BF16).astype(F32)
    return jnp.concatenate([upper, value - upper], axis=0).astype(BF16)


def iota(shape, dim):
    return lax.broadcasted_iota(jnp.int32, shape, dim)


def next_cell(x):
    shape = x.shape
    rolled = pltpu.roll(x, 127, 1)
    carried = pltpu.roll(rolled, shape[0] - 2, 0)
    carried = jnp.where(iota(shape, 0) >= shape[0] - 2, 0.0, carried)
    return jnp.where(iota(shape, 1) == 127, carried, rolled)


def previous_cell(x):
    shape = x.shape
    rolled = pltpu.roll(x, 1, 1)
    carried = pltpu.roll(rolled, 2, 0)
    carried = jnp.where(iota(shape, 0) < 2, 0.0, carried)
    return jnp.where(iota(shape, 1) == 0, carried, rolled)


def coupling_of(differ):
    d = differ.astype(F32)
    angle = d * (jnp.pi / 8)
    same = differ == 0
    sine = jnp.where(same, 1.0, jnp.sin(angle))
    return jnp.where(same, 0.0, 0.5 * jnp.cos(jnp.pi * d) * jnp.cos(angle) / sine)


def kernel(
    adj_h, adjw_h, jc_h, jl_h, jr_h, jcw_h, jlw_h, jrw_h, vol_h, volw_h, nrm_h, surf_h, imap_h, shp_h, damp_h, inv_h,
    flow_o, mesh_o, modal_o,
    adj, jac4, jac, vol, volw, nrm, surf, imap, shp, damp, inv,
    vol2, wf, w16, shi, slo, fl, fr, fb,
    ma, vm, abuf, xl, xp, mb, bbuf, rr, mm, halo,
    lsem, csem, ready,
    asend, arecv, hsend, hrecv, gsend, grecv, bsend, brecv,
):
    space, y = lax.axis_index("space"), lax.axis_index("inst")
    core = lax.rem(space, NC)
    chip = space // NC
    x = lax.rem(chip, NX)
    z = chip // NX
    other = 1 - core

    def at(zz, xx, cc):
        return (zz * NX + xx) * NC + cc

    def bring(src, dst, sem):
        copy = pltpu.make_async_copy(src, dst, sem)
        copy.start()
        return copy

    def together(ref, sem):
        pltpu.make_async_copy(ref, ref, sem).wait()

    for i, part in enumerate((jcw_h.at[:, 4], jlw_h.at[:, 4], jrw_h.at[:, 4], adjw_h)):
        bring(part, jac4.at[i], lsem.at[0])
    c_first = [bring(volw_h, volw, lsem.at[1]), bring(surf_h, surf, lsem.at[2]), bring(nrm_h, nrm, lsem.at[3])]

    def chunk(k):
        part = pl.ds(pl.multiple_of(k * CW, CW), CW)
        return pltpu.make_async_copy(shp_h.at[:, :, part], shp.at[:, pl.ds(0, MODES), part], csem.at[k])

    for k in range(AHEAD):
        chunk(k).start()

    barrier = pltpu.get_barrier_semaphore()

    def greet(where, inst):
        pl.semaphore_signal(barrier, inc=1, device_id=(where, inst), device_id_type=MESH)

    for dy in range(1, NY):
        for cc in range(NC):
            greet(at(z, x, cc), lax.rem(y + dy, NY))
    for dx in range(1, NX):
        greet(at(z, lax.rem(x + dx, NX), core), y)
    for dz in range(1, NZ):
        greet(at(lax.rem(z + dz, NZ), x, core), y)
    greet(at(z, x, other), y)
    greet(lax.rem(chip + CHIPS - 1, CHIPS) * NC + 1, y)
    greet(lax.rem(chip + 1, CHIPS) * NC, y)
    greeted = (NY - 1) * NC + (NX - 1) + (NZ - 1) + 3

    ma[...] = jnp.zeros_like(ma)
    vm[...] = jnp.zeros_like(vm)
    wf[...] = jnp.zeros_like(wf)
    for d in range(3):
        shp[d, pl.ds(MODES, ROWS - MODES), :] = jnp.zeros((ROWS - MODES, CELLS), F32)

    together(jac4, lsem.at[0])
    for c in c_first:
        c.wait()

    def direct4(i):
        total = jac4[i, 0] * jac4[3, 0]
        for f in range(1, 5):
            total = total + jac4[i, f] * jac4[3, f]
        return total

    left4, right4 = direct4(1), direct4(2)
    cell = iota((2, CELLS), 1)
    base4 = direct4(0) + jnp.where(cell == CELLS - 1, 0.0, pltpu.roll(left4, CELLS - 1, 1))
    base4 = base4 + jnp.where(cell == 0, 0.0, pltpu.roll(right4, 1, 1))
    late4 = volw[...] * jac4[3, 4]
    walls = surf[...].astype(F32)
    for d in range(3):
        part = pl.ds(d * CELLS, CELLS)
        g = nrm[pl.ds(d, 1), :] * walls
        wf[pl.ds(0, 2), part] = base4 * g
        wf[pl.ds(2, 2), part] = late4 * g
        wf[pl.ds(4, 1), pl.ds(d * CELLS, 128)] = jnp.where(iota((1, 128), 1) == 0, g[:, 0:128], 0.0)
        wf[pl.ds(5, 1), pl.ds((d + 1) * CELLS - 128, 128)] = jnp.where(iota((1, 128), 1) == 127, g[:, CELLS - 128 :], 0.0)
    w16[...] = halves(wf[...])

    across = (((1,), (1,)), ((), ()))

    def project(k, carry):
        chunk(k).wait()
        if AHEAD < CHUNKS:

            @pl.when(k + AHEAD < CHUNKS)
            def _():
                chunk(k + AHEAD).start()

        high, low = carry
        for d in range(3):
            part = pl.ds(pl.multiple_of(k * CW, CW), CW)
            tile = shp[d, :, part]
            upper = tile.astype(BF16)
            lower = (tile - upper.astype(F32)).astype(BF16)
            shi[d, :, part] = upper
            slo[d, :, part] = lower
            weight = w16[:, pl.ds(pl.multiple_of(d * CELLS + k * CW, CW), CW)]
            high = high + lax.dot_general(weight, upper, across, preferred_element_type=F32)
            low = low + lax.dot_general(weight, lower, across, preferred_element_type=F32)
        return high, low

    nothing = jnp.zeros((16, ROWS), F32)
    high, low = lax.fori_loop(0, CHUNKS, project, (nothing, nothing))
    both = high + low
    summed = both[0:8] + both[8:16]
    ma[:, pl.ds(0, ROWS)] = summed[0:4]
    vm[pl.ds(0, 2), pl.ds(0, ROWS)] = summed[4:6]
    lanes = iota((2, 128), 1)
    tail = ma[pl.ds(0, 2), pl.ds(128, 128)]
    tail = jnp.where(lanes == MODES - 128, left4[:, 0:1], tail)
    tail = jnp.where(lanes == MODES + 1 - 128, right4[:, CELLS - 1 :], tail)
    ma[pl.ds(0, 2), pl.ds(128, 128)] = tail

    for i, part in enumerate((jc_h, jl_h, jr_h)):
        bring(part, jac.at[i], csem.at[0])
    c_adj = [bring(adj_h, adj.at[y], csem.at[1]), bring(vol_h, vol, csem.at[2])]
    c_small = [bring(imap_h, imap, lsem.at[1]), bring(damp_h, damp, lsem.at[2]), bring(inv_h, inv, lsem.at[3])]
    pl.semaphore_wait(barrier, greeted)
    for dx in range(1, NX):
        pl.semaphore_signal(ready, inc=1, device_id=(at(z, lax.rem(x + dx, NX), core), y), device_id_type=MESH)

    def send(src, dst, ssem, rsem, where, inst):
        copy = pltpu.make_async_remote_copy(
            src_ref=src, dst_ref=dst, send_sem=ssem, recv_sem=rsem, device_id=(where, inst), device_id_type=MESH
        )
        copy.start()
        return copy

    mine = y * NC + core
    for dy, dc in ((2, 0), (2, 1), (1, 0), (3, 0), (1, 1), (3, 1), (0, 1)):
        cc = lax.rem(core + dc, NC)
        send(ma, abuf.at[mine], asend, arecv, at(z, x, cc), lax.rem(y + dy, NY))
    edge = NY * NC
    send(vm, abuf.at[edge + core], asend, arecv, at(z, x, other), y)
    outer = lax.rem(chip + 2 * core - 1 + CHIPS, CHIPS)
    for cc in range(NC):
        send(vm, abuf.at[edge + 3 - core], asend, arecv, outer * NC + cc, y)
    abuf[pl.ds(mine, 1)] = ma[...][None]
    abuf[pl.ds(edge + core, 1)] = vm[...][None]

    together(jac, csem.at[0])
    for c in c_adj:
        c.wait()
    for s in range(2):
        vol2[pl.ds(s, CT, stride=2), :] = vol[...]
    for dy in range(1, NY):
        send(adj.at[y], adj.at[y], gsend, grecv, space, lax.rem(y + dy, NY))

    def combine(j, e):
        total = j[0, e] * adj[y, 0]
        for f in range(1, 5):
            total = total + j[f, e] * adj[y, f]
        return total

    def component(e, carry):
        left, right = combine(jac.at[1], e), combine(jac.at[2], e)
        fl[e] = left
        fr[e] = right
        fb[e] = combine(jac.at[0], e) + next_cell(left) + previous_cell(right)
        return carry

    lax.fori_loop(0, 5, component, 0)
    before, after = lax.rem(space + TILES - 1, TILES), lax.rem(space + 1, TILES)
    send(fl.at[:, pl.ds(0, 8), :], halo.at[0], hsend, hrecv, before, y)
    send(fr.at[:, pl.ds(24, 8), :], halo.at[1], hsend, hrecv, after, y)

    for c in c_small:
        c.wait()
    eight = iota((8, 8), 0) == iota((8, 8), 1)
    slots = jnp.broadcast_to(imap[...], (8, 8))
    down = jnp.sum(jnp.where(eight, slots.astype(F32), 0.0), axis=1, keepdims=True)
    differ = jnp.broadcast_to(down, (8, 8)) - slots.astype(F32)
    h = coupling_of(differ.astype(jnp.int32))
    lanes8 = iota((8, 8), 1)

    def column_of(s):
        return jnp.sum(jnp.where(lanes8 == 2 * y + s, h, 0.0), axis=1, keepdims=True)

    pick = [column_of(s) for s in range(2)]

    together(abuf.at[pl.ds(0, NY * NC - 1 + 3)], arecv)
    for cc in range(NC):
        for yy in range(NY):
            xl[cc, pl.ds(2 * yy, 2), :] = abuf[yy * NC + cc, pl.ds(0, 2), :]
            xp[cc, pl.ds(2 * yy, 2), :] = abuf[yy * NC + cc, pl.ds(2, 2), :]
    has_before = jnp.where(chip > 0, 1.0, 0.0)
    has_after = jnp.where(chip < CHIPS - 1, 1.0, 0.0)
    proj = xl[0] + xl[1]
    edges = (
        (xl[0][:, 200:201] * has_before, abuf[edge + 2, pl.ds(1, 1), :]),
        (xl[0][:, 201:202], abuf[edge + 1, pl.ds(0, 1), :]),
        (xl[1][:, 200:201], abuf[edge, pl.ds(1, 1), :]),
        (xl[1][:, 201:202] * has_after, abuf[edge + 3, pl.ds(0, 1), :]),
    )
    for amount, vector in edges:
        proj = proj + amount * vector
    late = xp[0] + xp[1]
    for a in range(8):
        proj = proj - h[:, a : a + 1] * late[a : a + 1, :]
    mb[...] = jnp.zeros_like(mb)
    for s in range(2):
        plain = jnp.sum(jnp.where(iota((8, WIDE), 0) == 2 * y + s, proj, 0.0), axis=0, keepdims=True)
        mixed = jnp.sum(pick[s] * proj, axis=0, keepdims=True)
        rhs = plain[:, 0:MODES] + damp[...] * mixed[:, 0:MODES]
        mb[pl.ds(s, 1), :] = rhs[:, 0:128]
        mb[pl.ds(2 + s, 1), pl.ds(0, MODES - 128)] = rhs[:, 128:MODES]

    pl.semaphore_wait(ready, NX - 1)

    def hops(offset):
        dz, dx = offset
        return min(dz, NZ - dz) + min(dx, NX - dx)

    offsets = [(dz, dx) for dz in range(NZ) for dx in range(NX)][1:]
    for dz, dx in sorted(offsets, key=hops, reverse=True):
        where = at(lax.rem(z + dz, NZ), lax.rem(x + dx, NX), core)
        send(mb, bbuf.at[chip], bsend, brecv, where, y)
    bbuf[pl.ds(chip, 1)] = mb[...][None]

    rr[...] = jnp.zeros_like(rr)
    mm[...] = jnp.zeros_like(mm)
    together(halo, hrecv)
    together(adj.at[pl.ds(0, NY - 1)], grecv)
    lane8, sub8 = iota((8, 128), 1), iota((8, 128), 0)
    parity = lax.rem(sub8, 2)

    def entry(a, s):
        return jnp.broadcast_to(pick[s][a : a + 1, :], (8, 128))

    same = [jnp.where(parity == 0, entry(2 * yy, 0), entry(2 * yy + 1, 1)) for yy in range(NY)]
    cross = [jnp.where(parity == 0, entry(2 * yy + 1, 0), entry(2 * yy, 1)) for yy in range(NY)]
    follows = jnp.where(space < TILES - 1, 1.0, 0.0)
    leads = jnp.where(space > 0, 1.0, 0.0)

    def finish(e, carry):
        for q in range(4):
            part = pl.ds(8 * q, 8)
            timed = jnp.zeros((8, 128), F32)
            for yy in range(NY):
                here = adj[yy, e, part, :]
                swapped = jnp.where(parity == 0, pltpu.roll(here, 7, 0), pltpu.roll(here, 1, 0))
                timed = timed + here * same[yy] + swapped * cross[yy]
            total = fb[e, part, :] + vol2[part, :] * timed
            if q == 0:
                moved = pltpu.roll(pltpu.roll(halo[1, e], 1, 1), 2, 0)
                total = total + jnp.where((sub8 < 2) & (lane8 == 0), moved * leads, 0.0)
            if q == 3:
                moved = pltpu.roll(pltpu.roll(halo[0, e], 127, 1), 6, 0)
                total = total + jnp.where((sub8 >= 6) & (lane8 == 127), moved * follows, 0.0)
            flow_o[e, part, :] = total
        return carry

    lax.fori_loop(0, 5, finish, 0)
    together(abuf.at[pl.ds(0, NY * NC - 1 + 3)], asend)
    together(adj.at[pl.ds(0, NY - 1)], gsend)
    together(halo, hsend)

    together(bbuf.at[pl.ds(0, CHIPS - 1)], brecv)
    parts = [bbuf[n] for n in range(CHIPS)]
    while len(parts) > 1:
        parts = [parts[i] + parts[i + 1] for i in range(0, len(parts), 2)]
    total = parts[0]
    rr[pl.ds(0, 2), pl.ds(0, 128)] = total[0:2]
    rr[pl.ds(0, 2), pl.ds(128, 128)] = total[2:4]
    modal = jnp.dot(rr[:, pl.ds(0, MODES)], inv[...], precision=HIGHEST, preferred_element_type=F32)
    modal_o[...] = modal[0:2]
    mm[:, pl.ds(0, MODES)] = modal
    lead = halves(mm[:, pl.ds(0, ROWS)])
    plain_dot = (((1,), (0,)), ((), ()))
    for d in range(3):
        for k in range(CELLS // EW):
            part = pl.ds(k * EW, EW)
            spread = lax.dot_general(lead, shi[d, :, part], plain_dot, preferred_element_type=F32)
            spread = spread + lax.dot_general(lead, slo[d, :, part], plain_dot, preferred_element_type=F32)
            mesh_o[d, :, part] = (spread[0:8] + spread[8:16])[0:2] * surf[:, part].astype(F32)

    together(bbuf.at[pl.ds(0, CHIPS - 1)], bsend)


def place(*refs):
    copies = [pltpu.make_async_copy(refs[i], refs[3 + i], refs[6].at[i]) for i in range(3)]
    for copy in copies:
        copy.start()
    for copy in copies:
        copy.wait()


def shards(
    adjoint, jac_cell, jac_left, jac_right, volume, normals, surface, instance_map, mode_shapes, damping, modal_inverse
):
    def tiles(array):
        lead = array.shape[1:-1]
        n = len(lead)
        split = array.reshape((2,) + lead + (CT, 128))
        order = tuple(range(1, n + 1)) + (n + 1, 0, n + 2)
        return split.transpose(order).reshape(lead + (2 * CT, 128))

    def slots(array):
        lead = array.shape[0]
        return array.reshape(lead, CT, 2, 128).transpose(2, 0, 1, 3).reshape(2, lead, CT * 128)

    def wide(array):
        return jnp.moveaxis(array, 0, -2)

    args = (
        tiles(adjoint),
        wide(adjoint),
        tiles(jac_cell),
        tiles(jac_left),
        tiles(jac_right),
        wide(jac_cell),
        wide(jac_left),
        wide(jac_right),
        volume.reshape(CT, 128),
        volume.reshape(1, CELLS),
        normals,
        surface.reshape(1, CELLS),
        instance_map.reshape(1, 8),
        mode_shapes.transpose(1, 0, 2),
        damping.reshape(1, MODES),
        modal_inverse,
    )
    vmem = pltpu.VMEM
    results = ((5, 2 * CT, 128), (3, 2, CELLS), (2, MODES))
    dma = pltpu.SemaphoreType.DMA
    flow, mesh, modal = pl.pallas_call(
        kernel,
        out_shape=tuple(vmem(shape, F32) for shape in results),
        in_specs=[pl.BlockSpec(memory_space=pl.ANY)] * len(args),
        out_specs=[pl.BlockSpec(memory_space=pltpu.VMEM)] * 3,
        scratch_shapes=[
            vmem((NY, 5, 32, 128), F32),
            vmem((4, 5, 2, CELLS), F32),
            vmem((3, 5, 5, 32, 128), F32),
            vmem((CT, 128), F32),
            vmem((1, CELLS), F32),
            vmem((3, CELLS), F32),
            vmem((1, CELLS), jnp.int32),
            vmem((1, 8), jnp.int32),
            vmem((3, ROWS, CELLS), F32),
            vmem((1, MODES), F32),
            vmem((MODES, MODES), F32),
            vmem((32, 128), F32),
            vmem((8, 3 * CELLS), F32),
            vmem((16, 3 * CELLS), BF16),
            vmem((3, ROWS, CELLS), BF16),
            vmem((3, ROWS, CELLS), BF16),
            vmem((5, 32, 128), F32),
            vmem((5, 32, 128), F32),
            vmem((5, 32, 128), F32),
            vmem((4, WIDE), F32),
            vmem((4, WIDE), F32),
            vmem((NY * NC + 4, 4, WIDE), F32),
            vmem((2, 8, WIDE), F32),
            vmem((2, 8, WIDE), F32),
            vmem((4, 128), F32),
            vmem((CHIPS, 4, 128), F32),
            vmem((8, WIDE), F32),
            vmem((8, WIDE), F32),
            vmem((2, 5, 8, 128), F32),
            dma((4,)),
            dma((CHUNKS,)),
            pltpu.SemaphoreType.REGULAR,
        ]
        + [dma] * 8,
        compiler_params=pltpu.CompilerParams(
            collective_id=0, has_side_effects=True, vmem_limit_bytes=56 * 1024 * 1024
        ),
    )(*args)
    flow, mesh, modal = pl.pallas_call(
        place,
        out_shape=tuple(jax.ShapeDtypeStruct(shape, F32) for shape in results),
        in_specs=[pl.BlockSpec(memory_space=pltpu.VMEM)] * 3,
        out_specs=[pl.BlockSpec(memory_space=pltpu.HBM)] * 3,
        scratch_shapes=[dma((3,))],
    )(*(pltpu.with_memory_space_constraint(part, pltpu.VMEM) for part in (flow, mesh, modal)))
    return slots(flow), mesh.transpose(1, 0, 2), modal


def solution(mesh):
    placed = (
        P("inst", None, "space"),
        P("inst", None, None, "space"),
        P("inst", None, None, "space"),
        P("inst", None, None, "space"),
        P("space"),
        P(None, "space"),
        P("space"),
        P(),
        P(None, None, "space"),
        P(),
        P(),
    )
    return jax.shard_map(
        shards,
        mesh=mesh,
        in_specs=placed,
        out_specs=(P("inst", None, "space"), P("inst", None, "space"), P("inst", None)),
        check_vma=False,
    )
```

```python
import jax
import jax.numpy as jnp
from jax import lax
from jax.experimental import pallas as pl
from jax.experimental.pallas import tpu as pltpu
from jax.sharding import PartitionSpec as P

MESH = pl.DeviceIdType.MESH
HIGHEST = lax.Precision.HIGHEST
F32 = jnp.float32

NZ, NX, NY, NC = 8, 4, 4, 2
TILES = NZ * NX * NC
CHIPS = NZ * NX
MODES = 200
ROWS = 208
WIDE = 256
CT = 16
CELLS = CT * 128
CHUNKS = 4
AHEAD = 4
CW = CELLS // CHUNKS
EW = 1024
BF16 = jnp.bfloat16


def halves(value):
    upper = value.astype(BF16).astype(F32)
    return jnp.concatenate([upper, value - upper], axis=0).astype(BF16)


def iota(shape, dim):
    return lax.broadcasted_iota(jnp.int32, shape, dim)


def next_cell(x):
    shape = x.shape
    rolled = pltpu.roll(x, 127, 1)
    carried = pltpu.roll(rolled, shape[0] - 2, 0)
    carried = jnp.where(iota(shape, 0) >= shape[0] - 2, 0.0, carried)
    return jnp.where(iota(shape, 1) == 127, carried, rolled)


def previous_cell(x):
    shape = x.shape
    rolled = pltpu.roll(x, 1, 1)
    carried = pltpu.roll(rolled, 2, 0)
    carried = jnp.where(iota(shape, 0) < 2, 0.0, carried)
    return jnp.where(iota(shape, 1) == 0, carried, rolled)


def coupling_of(differ):
    d = differ.astype(F32)
    angle = d * (jnp.pi / 8)
    same = differ == 0
    sine = jnp.where(same, 1.0, jnp.sin(angle))
    return jnp.where(same, 0.0, 0.5 * jnp.cos(jnp.pi * d) * jnp.cos(angle) / sine)


def kernel(
    adj_h, adjw_h, jc_h, jl_h, jr_h, jcw_h, jlw_h, jrw_h, vol_h, volw_h, nrm_h, surf_h, imap_h, shp_h, damp_h, inv_h,
    flow_o, mesh_o, modal_o,
    adj, jac4, jac, vol, volw, nrm, surf, imap, shp, damp, inv,
    vol2, wf, w16, shi, slo, fl, fr, fb,
    ma, vm, abuf, xl, xp, mb, bbuf, rr, mm, halo,
    lsem, csem, ready,
    asend, arecv, hsend, hrecv, gsend, grecv, bsend, brecv,
):
    space, y = lax.axis_index("space"), lax.axis_index("inst")
    core = lax.rem(space, NC)
    chip = space // NC
    x = lax.rem(chip, NX)
    z = chip // NX
    other = 1 - core

    def at(zz, xx, cc):
        return (zz * NX + xx) * NC + cc

    def bring(src, dst, sem):
        copy = pltpu.make_async_copy(src, dst, sem)
        copy.start()
        return copy

    def together(ref, sem):
        pltpu.make_async_copy(ref, ref, sem).wait()

    for i, part in enumerate((jcw_h.at[:, 4], jlw_h.at[:, 4], jrw_h.at[:, 4], adjw_h)):
        bring(part, jac4.at[i], lsem.at[0])
    c_first = [bring(volw_h, volw, lsem.at[1]), bring(surf_h, surf, lsem.at[2]), bring(nrm_h, nrm, lsem.at[3])]

    def chunk(k):
        part = pl.ds(pl.multiple_of(k * CW, CW), CW)
        return pltpu.make_async_copy(shp_h.at[:, :, part], shp.at[:, pl.ds(0, MODES), part], csem.at[k])

    for k in range(AHEAD):
        chunk(k).start()

    barrier = pltpu.get_barrier_semaphore()

    def greet(where, inst):
        pl.semaphore_signal(barrier, inc=1, device_id=(where, inst), device_id_type=MESH)

    for dy in range(1, NY):
        for cc in range(NC):
            greet(at(z, x, cc), lax.rem(y + dy, NY))
    for dx in range(1, NX):
        greet(at(z, lax.rem(x + dx, NX), core), y)
    for dz in range(1, NZ):
        greet(at(lax.rem(z + dz, NZ), x, core), y)
    greet(at(z, x, other), y)
    greet(lax.rem(chip + CHIPS - 1, CHIPS) * NC + 1, y)
    greet(lax.rem(chip + 1, CHIPS) * NC, y)
    greeted = (NY - 1) * NC + (NX - 1) + (NZ - 1) + 3

    ma[...] = jnp.zeros_like(ma)
    vm[...] = jnp.zeros_like(vm)
    wf[...] = jnp.zeros_like(wf)
    for d in range(3):
        shp[d, pl.ds(MODES, ROWS - MODES), :] = jnp.zeros((ROWS - MODES, CELLS), F32)

    together(jac4, lsem.at[0])
    for c in c_first:
        c.wait()

    def direct4(i):
        total = jac4[i, 0] * jac4[3, 0]
        for f in range(1, 5):
            total = total + jac4[i, f] * jac4[3, f]
        return total

    left4, right4 = direct4(1), direct4(2)
    cell = iota((2, CELLS), 1)
    base4 = direct4(0) + jnp.where(cell == CELLS - 1, 0.0, pltpu.roll(left4, CELLS - 1, 1))
    base4 = base4 + jnp.where(cell == 0, 0.0, pltpu.roll(right4, 1, 1))
    late4 = volw[...] * jac4[3, 4]
    walls = surf[...].astype(F32)
    for d in range(3):
        part = pl.ds(d * CELLS, CELLS)
        g = nrm[pl.ds(d, 1), :] * walls
        wf[pl.ds(0, 2), part] = base4 * g
        wf[pl.ds(2, 2), part] = late4 * g
        wf[pl.ds(4, 1), pl.ds(d * CELLS, 128)] = jnp.where(iota((1, 128), 1) == 0, g[:, 0:128], 0.0)
        wf[pl.ds(5, 1), pl.ds((d + 1) * CELLS - 128, 128)] = jnp.where(iota((1, 128), 1) == 127, g[:, CELLS - 128 :], 0.0)
    w16[...] = halves(wf[...])

    across = (((1,), (1,)), ((), ()))

    def project(k, carry):
        chunk(k).wait()
        if AHEAD < CHUNKS:

            @pl.when(k + AHEAD < CHUNKS)
            def _():
                chunk(k + AHEAD).start()

        high, low = carry
        for d in range(3):
            part = pl.ds(pl.multiple_of(k * CW, CW), CW)
            tile = shp[d, :, part]
            upper = tile.astype(BF16)
            lower = (tile - upper.astype(F32)).astype(BF16)
            shi[d, :, part] = upper
            slo[d, :, part] = lower
            weight = w16[:, pl.ds(pl.multiple_of(d * CELLS + k * CW, CW), CW)]
            high = high + lax.dot_general(weight, upper, across, preferred_element_type=F32)
            low = low + lax.dot_general(weight, lower, across, preferred_element_type=F32)
        return high, low

    nothing = jnp.zeros((16, ROWS), F32)
    high, low = lax.fori_loop(0, CHUNKS, project, (nothing, nothing))
    both = high + low
    summed = both[0:8] + both[8:16]
    ma[:, pl.ds(0, ROWS)] = summed[0:4]
    vm[pl.ds(0, 2), pl.ds(0, ROWS)] = summed[4:6]
    lanes = iota((2, 128), 1)
    tail = ma[pl.ds(0, 2), pl.ds(128, 128)]
    tail = jnp.where(lanes == MODES - 128, left4[:, 0:1], tail)
    tail = jnp.where(lanes == MODES + 1 - 128, right4[:, CELLS - 1 :], tail)
    ma[pl.ds(0, 2), pl.ds(128, 128)] = tail

    for i, part in enumerate((jc_h, jl_h, jr_h)):
        bring(part, jac.at[i], csem.at[0])
    c_adj = [bring(adj_h, adj.at[y], csem.at[1]), bring(vol_h, vol, csem.at[2])]
    c_small = [bring(imap_h, imap, lsem.at[1]), bring(damp_h, damp, lsem.at[2]), bring(inv_h, inv, lsem.at[3])]
    pl.semaphore_wait(barrier, greeted)
    for dx in range(1, NX):
        pl.semaphore_signal(ready, inc=1, device_id=(at(z, lax.rem(x + dx, NX), core), y), device_id_type=MESH)

    def send(src, dst, ssem, rsem, where, inst):
        copy = pltpu.make_async_remote_copy(
            src_ref=src, dst_ref=dst, send_sem=ssem, recv_sem=rsem, device_id=(where, inst), device_id_type=MESH
        )
        copy.start()
        return copy

    mine = y * NC + core
    for dy, dc in ((2, 0), (2, 1), (1, 0), (3, 0), (1, 1), (3, 1), (0, 1)):
        cc = lax.rem(core + dc, NC)
        send(ma, abuf.at[mine], asend, arecv, at(z, x, cc), lax.rem(y + dy, NY))
    edge = NY * NC
    send(vm, abuf.at[edge + core], asend, arecv, at(z, x, other), y)
    outer = lax.rem(chip + 2 * core - 1 + CHIPS, CHIPS)
    for cc in range(NC):
        send(vm, abuf.at[edge + 3 - core], asend, arecv, outer * NC + cc, y)
    abuf[pl.ds(mine, 1)] = ma[...][None]
    abuf[pl.ds(edge + core, 1)] = vm[...][None]

    together(jac, csem.at[0])
    for c in c_adj:
        c.wait()
    for s in range(2):
        vol2[pl.ds(s, CT, stride=2), :] = vol[...]
    for dy in range(1, NY):
        send(adj.at[y], adj.at[y], gsend, grecv, space, lax.rem(y + dy, NY))

    def combine(j, e):
        total = j[0, e] * adj[y, 0]
        for f in range(1, 5):
            total = total + j[f, e] * adj[y, f]
        return total

    def component(e, carry):
        left, right = combine(jac.at[1], e), combine(jac.at[2], e)
        fl[e] = left
        fr[e] = right
        fb[e] = combine(jac.at[0], e) + next_cell(left) + previous_cell(right)
        return carry

    lax.fori_loop(0, 5, component, 0)
    before, after = lax.rem(space + TILES - 1, TILES), lax.rem(space + 1, TILES)
    send(fl.at[:, pl.ds(0, 8), :], halo.at[0], hsend, hrecv, before, y)
    send(fr.at[:, pl.ds(24, 8), :], halo.at[1], hsend, hrecv, after, y)

    for c in c_small:
        c.wait()
    eight = iota((8, 8), 0) == iota((8, 8), 1)
    slots = jnp.broadcast_to(imap[...], (8, 8))
    down = jnp.sum(jnp.where(eight, slots.astype(F32), 0.0), axis=1, keepdims=True)
    differ = jnp.broadcast_to(down, (8, 8)) - slots.astype(F32)
    h = coupling_of(differ.astype(jnp.int32))
    lanes8 = iota((8, 8), 1)

    def column_of(s):
        return jnp.sum(jnp.where(lanes8 == 2 * y + s, h, 0.0), axis=1, keepdims=True)

    pick = [column_of(s) for s in range(2)]

    together(abuf.at[pl.ds(0, NY * NC - 1 + 3)], arecv)
    for cc in range(NC):
        for yy in range(NY):
            xl[cc, pl.ds(2 * yy, 2), :] = abuf[yy * NC + cc, pl.ds(0, 2), :]
            xp[cc, pl.ds(2 * yy, 2), :] = abuf[yy * NC + cc, pl.ds(2, 2), :]
    has_before = jnp.where(chip > 0, 1.0, 0.0)
    has_after = jnp.where(chip < CHIPS - 1, 1.0, 0.0)
    proj = xl[0] + xl[1]
    edges = (
        (xl[0][:, 200:201] * has_before, abuf[edge + 2, pl.ds(1, 1), :]),
        (xl[0][:, 201:202], abuf[edge + 1, pl.ds(0, 1), :]),
        (xl[1][:, 200:201], abuf[edge, pl.ds(1, 1), :]),
        (xl[1][:, 201:202] * has_after, abuf[edge + 3, pl.ds(0, 1), :]),
    )
    for amount, vector in edges:
        proj = proj + amount * vector
    late = xp[0] + xp[1]
    for a in range(8):
        proj = proj - h[:, a : a + 1] * late[a : a + 1, :]
    mb[...] = jnp.zeros_like(mb)
    for s in range(2):
        plain = jnp.sum(jnp.where(iota((8, WIDE), 0) == 2 * y + s, proj, 0.0), axis=0, keepdims=True)
        mixed = jnp.sum(pick[s] * proj, axis=0, keepdims=True)
        rhs = plain[:, 0:MODES] + damp[...] * mixed[:, 0:MODES]
        mb[pl.ds(s, 1), :] = rhs[:, 0:128]
        mb[pl.ds(2 + s, 1), pl.ds(0, MODES - 128)] = rhs[:, 128:MODES]

    pl.semaphore_wait(ready, NX - 1)

    def hops(offset):
        dz, dx = offset
        return min(dz, NZ - dz) + min(dx, NX - dx)

    offsets = [(dz, dx) for dz in range(NZ) for dx in range(NX)][1:]
    for dz, dx in sorted(offsets, key=hops, reverse=True):
        where = at(lax.rem(z + dz, NZ), lax.rem(x + dx, NX), core)
        send(mb, bbuf.at[chip], bsend, brecv, where, y)
    bbuf[pl.ds(chip, 1)] = mb[...][None]

    rr[...] = jnp.zeros_like(rr)
    mm[...] = jnp.zeros_like(mm)
    together(halo, hrecv)
    together(adj.at[pl.ds(0, NY - 1)], grecv)
    lane8, sub8 = iota((8, 128), 1), iota((8, 128), 0)
    parity = lax.rem(sub8, 2)

    def entry(a, s):
        return jnp.broadcast_to(pick[s][a : a + 1, :], (8, 128))

    same = [jnp.where(parity == 0, entry(2 * yy, 0), entry(2 * yy + 1, 1)) for yy in range(NY)]
    cross = [jnp.where(parity == 0, entry(2 * yy + 1, 0), entry(2 * yy, 1)) for yy in range(NY)]
    follows = jnp.where(space < TILES - 1, 1.0, 0.0)
    leads = jnp.where(space > 0, 1.0, 0.0)

    def finish(e, carry):
        for q in range(4):
            part = pl.ds(8 * q, 8)
            timed = jnp.zeros((8, 128), F32)
            for yy in range(NY):
                here = adj[yy, e, part, :]
                swapped = jnp.where(parity == 0, pltpu.roll(here, 7, 0), pltpu.roll(here, 1, 0))
                timed = timed + here * same[yy] + swapped * cross[yy]
            total = fb[e, part, :] + vol2[part, :] * timed
            if q == 0:
                moved = pltpu.roll(pltpu.roll(halo[1, e], 1, 1), 2, 0)
                total = total + jnp.where((sub8 < 2) & (lane8 == 0), moved * leads, 0.0)
            if q == 3:
                moved = pltpu.roll(pltpu.roll(halo[0, e], 127, 1), 6, 0)
                total = total + jnp.where((sub8 >= 6) & (lane8 == 127), moved * follows, 0.0)
            flow_o[e, part, :] = total
        return carry

    lax.fori_loop(0, 5, finish, 0)
    together(abuf.at[pl.ds(0, NY * NC - 1 + 3)], asend)
    together(adj.at[pl.ds(0, NY - 1)], gsend)
    together(halo, hsend)

    together(bbuf.at[pl.ds(0, CHIPS - 1)], brecv)
    parts = [bbuf[n] for n in range(CHIPS)]
    while len(parts) > 1:
        parts = [parts[i] + parts[i + 1] for i in range(0, len(parts), 2)]
    total = parts[0]
    rr[pl.ds(0, 2), pl.ds(0, 128)] = total[0:2]
    rr[pl.ds(0, 2), pl.ds(128, 128)] = total[2:4]
    modal = jnp.dot(rr[:, pl.ds(0, MODES)], inv[...], precision=HIGHEST, preferred_element_type=F32)
    modal_o[...] = modal[0:2]
    mm[:, pl.ds(0, MODES)] = modal
    lead = halves(mm[:, pl.ds(0, ROWS)])
    plain_dot = (((1,), (0,)), ((), ()))
    for d in range(3):
        for k in range(CELLS // EW):
            part = pl.ds(k * EW, EW)
            spread = lax.dot_general(lead, shi[d, :, part], plain_dot, preferred_element_type=F32)
            spread = spread + lax.dot_general(lead, slo[d, :, part], plain_dot, preferred_element_type=F32)
            mesh_o[d, :, part] = (spread[0:8] + spread[8:16])[0:2] * surf[:, part].astype(F32)

    together(bbuf.at[pl.ds(0, CHIPS - 1)], bsend)


def place(*refs):
    copies = [pltpu.make_async_copy(refs[i], refs[3 + i], refs[6].at[i]) for i in range(3)]
    for copy in copies:
        copy.start()
    for copy in copies:
        copy.wait()


def shards(
    adjoint, jac_cell, jac_left, jac_right, volume, normals, surface, instance_map, mode_shapes, damping, modal_inverse
):
    def tiles(array):
        lead = array.shape[1:-1]
        n = len(lead)
        split = array.reshape((2,) + lead + (CT, 128))
        order = tuple(range(1, n + 1)) + (n + 1, 0, n + 2)
        return split.transpose(order).reshape(lead + (2 * CT, 128))

    def slots(array):
        lead = array.shape[0]
        return array.reshape(lead, CT, 2, 128).transpose(2, 0, 1, 3).reshape(2, lead, CT * 128)

    def wide(array):
        return jnp.moveaxis(array, 0, -2)

    args = (
        tiles(adjoint),
        wide(adjoint),
        tiles(jac_cell),
        tiles(jac_left),
        tiles(jac_right),
        wide(jac_cell),
        wide(jac_left),
        wide(jac_right),
        volume.reshape(CT, 128),
        volume.reshape(1, CELLS),
        normals,
        surface.reshape(1, CELLS),
        instance_map.reshape(1, 8),
        mode_shapes.transpose(1, 0, 2),
        damping.reshape(1, MODES),
        modal_inverse,
    )
    vmem = pltpu.VMEM
    results = ((5, 2 * CT, 128), (3, 2, CELLS), (2, MODES))
    dma = pltpu.SemaphoreType.DMA
    flow, mesh, modal = pl.pallas_call(
        kernel,
        out_shape=tuple(vmem(shape, F32) for shape in results),
        in_specs=[pl.BlockSpec(memory_space=pl.ANY)] * len(args),
        out_specs=[pl.BlockSpec(memory_space=pltpu.VMEM)] * 3,
        scratch_shapes=[
            vmem((NY, 5, 32, 128), F32),
            vmem((4, 5, 2, CELLS), F32),
            vmem((3, 5, 5, 32, 128), F32),
            vmem((CT, 128), F32),
            vmem((1, CELLS), F32),
            vmem((3, CELLS), F32),
            vmem((1, CELLS), jnp.int32),
            vmem((1, 8), jnp.int32),
            vmem((3, ROWS, CELLS), F32),
            vmem((1, MODES), F32),
            vmem((MODES, MODES), F32),
            vmem((32, 128), F32),
            vmem((8, 3 * CELLS), F32),
            vmem((16, 3 * CELLS), BF16),
            vmem((3, ROWS, CELLS), BF16),
            vmem((3, ROWS, CELLS), BF16),
            vmem((5, 32, 128), F32),
            vmem((5, 32, 128), F32),
            vmem((5, 32, 128), F32),
            vmem((4, WIDE), F32),
            vmem((4, WIDE), F32),
            vmem((NY * NC + 4, 4, WIDE), F32),
            vmem((2, 8, WIDE), F32),
            vmem((2, 8, WIDE), F32),
            vmem((4, 128), F32),
            vmem((CHIPS, 4, 128), F32),
            vmem((8, WIDE), F32),
            vmem((8, WIDE), F32),
            vmem((2, 5, 8, 128), F32),
            dma((4,)),
            dma((CHUNKS,)),
            pltpu.SemaphoreType.REGULAR,
        ]
        + [dma] * 8,
        compiler_params=pltpu.CompilerParams(
            collective_id=0, has_side_effects=True, vmem_limit_bytes=56 * 1024 * 1024
        ),
    )(*args)
    flow, mesh, modal = pl.pallas_call(
        place,
        out_shape=tuple(jax.ShapeDtypeStruct(shape, F32) for shape in results),
        in_specs=[pl.BlockSpec(memory_space=pltpu.VMEM)] * 3,
        out_specs=[pl.BlockSpec(memory_space=pltpu.HBM)] * 3,
        scratch_shapes=[dma((3,))],
    )(*(pltpu.with_memory_space_constraint(part, pltpu.VMEM) for part in (flow, mesh, modal)))
    return slots(flow), mesh.transpose(1, 0, 2), modal


def solution(mesh):
    placed = (
        P("inst", None, "space"),
        P("inst", None, None, "space"),
        P("inst", None, None, "space"),
        P("inst", None, None, "space"),
        P("space"),
        P(None, "space"),
        P("space"),
        P(),
        P(None, None, "space"),
        P(),
        P(),
    )
    return jax.shard_map(
        shards,
        mesh=mesh,
        in_specs=placed,
        out_specs=(P("inst", None, "space"), P("inst", None, "space"), P("inst", None)),
        check_vma=False,
    )
```
